256 devices in a mesh: sec: 32 (over x, y, core), mpo: 8 (over z).
Axes of the slice: x: 4, y: 4, z: 8, core: 2. Of those that a mesh axis runs over, the one named last changes fastest.
Arguments:
- guess: float32 [24576, 256], P('sec'), may hold values from -6 to 6
- left_env: bfloat16 [40, 24576, 768], P('mpo', 'sec'), may hold values from -0.21875 to 0.21875
- right_env: bfloat16 [40, 8192, 256], P('mpo', 'sec'), may hold values from -0.375 to 0.375
- block_rows: int32 [32], replicated, may hold values from 1 to 768, 8192 in all
- charges: int32 [40], P('mpo'), may hold values from -2 to 2, as said below
- ranks: int32 [32], replicated, may hold values from 1 to 256
Outputs:
- wavefunction: float32 [24576, 256], P(('sec', 'mpo'))
- truncated: float32 [24576, 256], P(('sec', 'mpo'))
The draws below stay inside these ranges and needn't reach their ends.
Inputs may be any that keep to these rules, and one draw needn't show every extreme that they name: The 5 terms of one index of mpo (each aligned run of 5 terms) carry the charges -2, -1, 0, 1, 2 once each.
All inputs are finite; a program needn't handle non-finite values.
Results may differ from the reference program's by a relative error of at most 0.01.
Values may be sent and summed in bfloat16 or wider, within the bound.
No kernel may reach another device: no remote copies, remote signals or barrier semaphores. Data moves between devices by JAX's collectives and lax.ppermute only.
A program may use at most 64 MiB of HBM per device.

```python
import math
import jax
import jax.numpy as jnp
import numpy as np
from jax import lax

MEAN = 256
RB = 256
ITERS = 4
CAP = 768
NSEC = 32
TERMS = 40


def draw_charges(key, part):
    subkeys = jax.random.split(jax.random.fold_in(key, 7), TERMS // 5)
    groups = jax.vmap(lambda subkey: jax.random.permutation(subkey, 5))(subkeys)
    return (groups.reshape(-1) - 2).astype(jnp.int32)


def place_ends(array, key, least, largest):
    place = [jax.random.randint(jax.random.fold_in(key, axis), (), 0, length) for axis, length in enumerate(array.shape)]
    main_axis = array.shape.index(max(array.shape))
    beside = place[:main_axis] + [(place[main_axis] + 1) % array.shape[main_axis]] + place[main_axis + 1:]
    return array.at[tuple(place)].set(least).at[tuple(beside)].set(largest)


def block_levels(rng, dims, pieces, smallest, largest):
    def one(position, shards_of):
        steps = jax.random.uniform(jax.random.fold_in(jax.random.fold_in(rng, 6), position), (shards_of,), jnp.float32, smallest / len(pieces), largest / len(pieces))
        return jnp.repeat(jnp.exp(steps), dims[position] // shards_of).reshape((-1,) + (1,) * (len(dims) - position - 1))

    gain = one(*pieces[0])
    for cut in pieces[1:]:
        gain = gain * one(*cut)
    return gain


def length_profile(amount, total, most, skew):
    loads = [(1 << 20) // math.isqrt(rank ** skew) + 1 for rank in range(2, amount + 1)]
    rest, given = total - most - (amount - 1), [1] * (amount - 1)
    while rest > 0:
        free = [i for i in range(amount - 1) if given[i] < most]
        whole, remaining = sum([loads[i] for i in free]), rest
        for i in free:
            addition = min(most - given[i], max(1, remaining * loads[i] // whole), rest)
            given[i] = given[i] + addition
            rest = rest - addition
    return np.array([most] + given)


def ragged(stream_key, amount, total, most, lean):
    if amount == 2:
        one = jax.random.randint(stream_key, (), max(1, total - most), min(most, total - 1) + 1)
        return jnp.stack([one, total - one])
    tallies = jnp.asarray(length_profile(amount, total, most, lean), jnp.int32)
    twos = (amount - 1) // 2
    giver, taker = tallies[1:1 + 2 * twos:2], tallies[2:2 + 2 * twos:2]
    room = jnp.minimum(giver - 1, most - taker)
    moved = jax.random.randint(jax.random.fold_in(stream_key, 1), (twos,), 0, 1 << 20) % (room + 1)
    tallies = tallies.at[1:1 + 2 * twos:2].set(giver - moved).at[2:2 + 2 * twos:2].set(taker + moved)
    return tallies[jax.random.permutation(jax.random.fold_in(stream_key, 2), amount)]


def normal_values(stream_key, extent, spread, most, cuts=(), held_as=jnp.bfloat16):
    loudness = block_levels(stream_key, extent, cuts, -0.22, 0.18) if cuts else 1.0
    drawn = jax.random.normal(stream_key, extent, jnp.float32) * spread * loudness
    return jnp.minimum(jnp.maximum(drawn, -most), most).astype(held_as)


def setup_inputs(seed: int = 0) -> dict:
    key_of = jax.random.split(jax.random.key(seed), 7)
    return {
        "guess": normal_values(key_of[0], (NSEC * CAP, RB), 1.0, 6.0, ((0, 32),), jnp.float32),
        "left_env": normal_values(key_of[1], (TERMS, NSEC * CAP, CAP), CAP ** -0.5, 0.21875, ((0, 8), (1, 32))),
        "right_env": normal_values(key_of[2], (TERMS, NSEC * RB, RB), RB ** -0.5, 0.375, ((0, 8), (1, 32))),
        "block_rows": ragged(key_of[3], NSEC, MEAN * NSEC, CAP, 2).astype(jnp.int32),
        "charges": draw_charges(jax.random.fold_in(key_of[6], 71), 0),
        "ranks": place_ends(jax.random.randint(key_of[5], (NSEC,), 1, RB + 1), jax.random.fold_in(key_of[5], 1), 1, RB).astype(jnp.int32),
    }


epsilon = 1e-06
step_size = 0.1
highest = lax.Precision.HIGHEST

def apply_operator(current, left_blocks, right_blocks, charges, row_mask):
    rounded = current.astype(jnp.bfloat16)

    def add_term(running, inputs):
        left_term, right_term, charge = inputs
        shifted = jnp.roll(rounded, charge, axis=0)
        middle = jnp.einsum('sij,sjk->sik', left_term.astype(jnp.float32), shifted.astype(jnp.float32)).astype(jnp.bfloat16)
        summand = jnp.einsum('sik,skl->sil', middle.astype(jnp.float32), right_term.astype(jnp.float32))
        return (running + summand, None)
    applied, unused = lax.scan(add_term, jnp.zeros(current.shape, jnp.float32), (left_blocks, right_blocks, charges))
    return applied * row_mask

def solve_block(lower_factor, right_side):
    return jax.scipy.linalg.cho_solve((lower_factor, True), right_side.T).T

def reference(guess, left_env, right_env, block_rows, charges, ranks):
    entries = MEAN * NSEC * RB
    positions = jnp.arange(CAP, dtype=jnp.int32)
    row_mask = (positions[None, :] < block_rows[:, None]).astype(jnp.float32)[:, :, None]
    current = guess.reshape(NSEC, CAP, RB) * row_mask
    current = current * lax.rsqrt(jnp.sum(current * current) / entries + epsilon)
    left_blocks = left_env.reshape(TERMS, NSEC, CAP, CAP)
    right_blocks = right_env.reshape(TERMS, NSEC, RB, RB)
    for repeat in range(ITERS):
        applied = apply_operator(current, left_blocks, right_blocks, charges.astype(jnp.int32), row_mask)
        rayleigh = jnp.sum(current * applied) / (jnp.sum(current * current) + epsilon)
        update = current - step_size * (applied - rayleigh * current)
        current = update * lax.rsqrt(jnp.sum(update * update) / entries + epsilon)
    density = jnp.einsum('sij,sik->sjk', current, current, precision=highest)
    columns = (jnp.arange(RB, dtype=jnp.int32)[None, :] < ranks[:, None]).astype(jnp.float32)
    span_basis = (jnp.eye(RB, dtype=jnp.float32)[None] + density / MEAN) * columns[:, None, :]
    gram_matrix = jnp.einsum('sij,sik->sjk', span_basis, span_basis, precision=highest) + jax.vmap(jnp.diag)(1.0 - columns)
    factor = jnp.linalg.cholesky(gram_matrix)
    coords = jnp.einsum('sij,sjk->sik', current, span_basis, precision=highest)
    solved = jax.vmap(solve_block)(factor, coords)
    truncated = jnp.einsum('sik,sjk->sij', solved, span_basis, precision=highest)
    return (current.reshape(NSEC * CAP, RB), truncated.reshape(NSEC * CAP, RB))
```

```python
import jax
import jax.numpy as jnp
from jax import lax
from jax.experimental import pallas as pl
from jax.experimental.pallas import tpu as pltpu
from jax.sharding import PartitionSpec as P

MEAN = 256
ITERS = 4
REACH = 2
SHRINK = 2.0**-7
epsilon = 1e-06
step_size = 0.1
highest = lax.Precision.HIGHEST
TILE = 256
BASE = 64


def sent_to_all(array, axis):
    peers = lax.axis_size(axis)
    return lax.all_to_all(
        jnp.broadcast_to(array[None], (peers, *array.shape)), axis, 0, 0, tiled=True
    )


def passed_along(array, axis, by):
    peers = lax.axis_size(axis)
    return lax.ppermute(array, axis, [(i, (i + by) % peers) for i in range(peers)])


def operator_body(rows_ref, charges_ref, *refs):
    blocks = refs[: 2 * REACH + 1]
    left_ref, right_ref, out_ref, held, total, sems = refs[2 * REACH + 1 :]
    term = pl.program_id(0)
    copies = [
        pltpu.make_async_copy(block, held.at[i], sems.at[i]) for i, block in enumerate(blocks)
    ]

    @pl.when(term == 0)
    def _():
        for copy in copies:
            copy.start()
        total[...] = jnp.zeros_like(total)
        for copy in copies:
            copy.wait()

    shift = charges_ref[term]
    own_rows = rows_ref[REACH]
    source_rows = rows_ref[REACH - shift]
    slot = REACH + shift
    tiles = held.shape[1] // TILE
    for i in range(tiles):
        for j in range(1, tiles + 1):
            low, high = (j - 1) * TILE, j * TILE
            fits = (own_rows > i * TILE) & (source_rows > low)
            if j < tiles:
                fits = fits & (source_rows <= high)

            @pl.when(fits)
            def _():
                span = pl.ds(i * TILE, TILE)
                middle = jnp.dot(
                    left_ref[0, span, :high],
                    held[slot, :high, :],
                    preferred_element_type=jnp.float32,
                ).astype(jnp.bfloat16)
                total[span, :] += jnp.dot(
                    middle, right_ref[0], preferred_element_type=jnp.float32
                )

    @pl.when(term == pl.num_programs(0) - 1)
    def _():
        row = lax.broadcasted_iota(jnp.int32, total.shape, 0)
        out_ref[...] = jnp.where(row < own_rows, total[...] * SHRINK, 0.0).astype(out_ref.dtype)


def apply_terms(rows, charges, blocks, left_env, right_env):
    terms, capacity, _ = left_env.shape
    width = right_env.shape[-1]
    count = len(blocks)
    return pl.pallas_call(
        operator_body,
        grid_spec=pltpu.PrefetchScalarGridSpec(
            num_scalar_prefetch=2,
            grid=(terms,),
            in_specs=[pl.BlockSpec(memory_space=pl.ANY)] * count
            + [
                pl.BlockSpec((1, capacity, capacity), lambda w, *_: (w, 0, 0)),
                pl.BlockSpec((1, width, width), lambda w, *_: (w, 0, 0)),
            ],
            out_specs=pl.BlockSpec((capacity, width), lambda w, *_: (0, 0)),
            scratch_shapes=[
                pltpu.VMEM((count, capacity, width), jnp.bfloat16),
                pltpu.VMEM((capacity, width), jnp.float32),
                pltpu.SemaphoreType.DMA((count,)),
            ],
        ),
        out_shape=jax.ShapeDtypeStruct((capacity, width), jnp.bfloat16),
        compiler_params=pltpu.CompilerParams(vmem_limit_bytes=40 << 20),
        name="apply_terms",
    )(rows, charges, *blocks, left_env, right_env)


PAIRS = [(i, j) for i in range(ITERS + 1) for j in range(i, ITERS + 1)]


def products_body(rows_ref, first_ref, *refs):
    powers, out_ref = refs[:-1], refs[-1]
    arrays = [first_ref[...]] + [ref[...].astype(jnp.float32) for ref in powers]
    lane = lax.broadcasted_iota(jnp.int32, (1, 128), 1)
    out = jnp.zeros((1, 128), jnp.float32)
    for place, (i, j) in enumerate(PAIRS):
        value = jnp.sum(jnp.sum(arrays[i] * arrays[j], axis=0, keepdims=True), axis=1, keepdims=True)
        out = out + jnp.where(lane == place, value, 0.0)
    out_ref[...] = out


def products(start, powers):
    return pl.pallas_call(
        lambda *refs: products_body(None, *refs),
        out_shape=jax.ShapeDtypeStruct((1, 128), jnp.float32),
        compiler_params=pltpu.CompilerParams(vmem_limit_bytes=40 << 20),
        name="products",
    )(start, *powers)


def dot32(a, b, dims):
    return lax.dot_general(
        a, b, (dims, ((), ())), precision=highest, preferred_element_type=jnp.float32
    )


def swept_block(block):
    size = block.shape[0]
    row = lax.broadcasted_iota(jnp.int32, block.shape, 0)
    lane = lax.broadcasted_iota(jnp.int32, block.shape, 1)
    for k in range(size):
        pivot_row = block[k : k + 1, :]
        pivot_col = block[:, k : k + 1]
        inverse = 1.0 / block[k : k + 1, k : k + 1]
        scaled = pivot_row * inverse
        update = block - pivot_col * scaled
        update = jnp.where(lane == k, pivot_col * inverse, update)
        update = jnp.where(row == k, scaled, update)
        block = jnp.where((row == k) & (lane == k), -inverse, update)
    return -block


def tail_body(info_ref, sums_ref, start_ref, *refs):
    powers = refs[:ITERS]
    slab_ref, cut_ref, state, gram = refs[ITERS:]
    entries = info_ref[2].astype(jnp.float32)
    summed = jnp.sum(sums_ref[...], axis=0, keepdims=True)
    table = {}
    for place, (i, j) in enumerate(PAIRS):
        table[i, j] = table[j, i] = summed[:, place : place + 1]

    def inner(a, b):
        out = 0.0
        for i, x in enumerate(a):
            for j, y in enumerate(b):
                if x is not None and y is not None:
                    out = out + x * y * table[i, j]
        return out

    def scale_of(squares):
        return lax.rsqrt(squares / entries + epsilon)

    weights = [scale_of(table[0, 0])] + [None] * ITERS
    for _ in range(ITERS):
        image = [None] + [None if x is None else x * (1.0 / SHRINK) for x in weights[:-1]]
        rayleigh = inner(weights, image) / (inner(weights, weights) + epsilon)
        update = []
        for x, y in zip(weights, image):
            value = None
            if x is not None:
                value = x * (1.0 + step_size * rayleigh)
            if y is not None:
                value = -step_size * y if value is None else value - step_size * y
            update.append(value)
        scale = scale_of(jnp.maximum(inner(update, update), 0.0))
        weights = [None if x is None else x * scale for x in update]

    current = weights[0] * start_ref[...]
    for weight, ref in zip(weights[1:], powers):
        current = current + weight * ref[...].astype(jnp.float32)
    state[...] = current
    density = dot32(current, current, ((0,), (0,)))
    width = density.shape[0]
    row = lax.broadcasted_iota(jnp.int32, density.shape, 0)
    lane = lax.broadcasted_iota(jnp.int32, density.shape, 1)
    diagonal = (row == lane).astype(jnp.float32)
    kept = lane < info_ref[1]
    basis = jnp.where(kept, diagonal + density * (1.0 / MEAN), 0.0)
    gram[...] = dot32(basis, basis, ((0,), (0,))) + jnp.where(kept, 0.0, diagonal)
    panel_row = lax.broadcasted_iota(jnp.int32, (BASE, width), 0)
    panel_lane = lax.broadcasted_iota(jnp.int32, (BASE, width), 1)
    for b in range(width // BASE):
        low = b * BASE
        panel = gram[low : low + BASE, :]
        inverse = swept_block(panel[:, low : low + BASE])
        inside = (panel_lane >= low) & (panel_lane < low + BASE)
        select = (panel_lane == panel_row + low).astype(jnp.float32)
        rest = jnp.where(inside, 0.0, panel)
        solved = dot32(inverse, rest, ((1,), (0,)))
        change = dot32(
            jnp.concatenate([rest, solved], axis=0),
            jnp.concatenate([solved, -select], axis=0),
            ((0,), (0,)),
        )
        held = (lane >= low) & (lane < low + BASE)
        gram[...] = jnp.where(held, 0.0, gram[...]) - change
        gram[low : low + BASE, :] = solved - dot32(inverse, select, ((1,), (0,)))
    slab_rows = slab_ref.shape[0]
    slab = state[pl.ds(pl.multiple_of(info_ref[0] * slab_rows, 8), slab_rows), :]
    slab_ref[...] = slab
    coords = dot32(slab, basis, ((1,), (0,)))
    solved = -dot32(coords, gram[...], ((1,), (0,)))
    cut_ref[...] = dot32(solved, basis, ((1,), (1,)))


def tail(info, sums, start, powers, slab_rows):
    capacity, width = start.shape
    vmem = pl.BlockSpec(memory_space=pltpu.VMEM)
    return pl.pallas_call(
        tail_body,
        in_specs=[pl.BlockSpec(memory_space=pltpu.SMEM)] + [vmem] * (2 + ITERS),
        out_shape=[jax.ShapeDtypeStruct((slab_rows, width), jnp.float32)] * 2,
        scratch_shapes=[
            pltpu.VMEM((capacity, width), jnp.float32),
            pltpu.VMEM((width, width), jnp.float32),
        ],
        compiler_params=pltpu.CompilerParams(vmem_limit_bytes=40 << 20),
        name="truncate",
    )(info, sums, start, *powers)


def shards(guess, left_env, right_env, block_rows, charges, ranks):
    capacity, width = guess.shape
    sectors = block_rows.shape[0]
    sector = lax.axis_index("sec")
    member = lax.axis_index("mpo")
    members = lax.axis_size("mpo")
    slab_rows = capacity // members
    rows = jnp.stack([block_rows[(sector + d) % sectors] for d in range(-REACH, REACH + 1)])
    own_rows = rows[REACH]
    start = jnp.where(jnp.arange(capacity, dtype=jnp.int32)[:, None] < own_rows, guess, 0.0)
    whole = start.astype(jnp.bfloat16)
    powers = []
    for repeat in range(ITERS):
        blocks = [
            whole if by == 0 else passed_along(whole, "sec", by)
            for by in range(-REACH, REACH + 1)
        ]
        part = apply_terms(rows, charges, blocks, left_env, right_env)
        pieces = lax.all_to_all(
            part.reshape(members, slab_rows, width), "mpo", 0, 0, tiled=True
        )
        slab = jnp.sum(pieces.astype(jnp.float32), axis=0).astype(jnp.bfloat16)
        whole = sent_to_all(slab, "mpo").reshape(capacity, width)
        powers.append(whole)
    sums = sent_to_all(products(start, powers), "sec").reshape(sectors, 128)
    info = jnp.stack([member, ranks[sector], MEAN * sectors * width]).astype(jnp.int32)
    slab, cut = tail(info, sums, start, powers, slab_rows)
    return (slab, cut)


def solution(mesh):
    return jax.shard_map(
        shards,
        mesh=mesh,
        in_specs=(P("sec", None), P("mpo", "sec", None), P("mpo", "sec", None), P(), P("mpo"), P()),
        out_specs=(P(("sec", "mpo"), None), P(("sec", "mpo"), None)),
        check_vma=False,
    )
```

```python
import jax
import jax.numpy as jnp
from jax import lax
from jax.experimental import pallas as pl
from jax.experimental.pallas import tpu as pltpu
from jax.sharding import PartitionSpec as P

MEAN = 256
ITERS = 4
REACH = 2
SHRINK = 2.0**-4
epsilon = 1e-06
step_size = 0.1
highest = lax.Precision.HIGHEST
TILE = 256
BASE = 64
EXTRA = 16
PAIRS = [(i, j) for i in range(ITERS + 1) for j in range(i, ITERS + 1)]
SMEM = pl.BlockSpec(memory_space=pltpu.SMEM)
VMEM = pl.BlockSpec(memory_space=pltpu.VMEM)


def call(body, name, out_shape, in_specs, scratch=(), limit=16):
    return pl.pallas_call(
        body,
        in_specs=in_specs,
        out_specs=jax.tree.map(lambda _: VMEM, out_shape),
        out_shape=out_shape,
        scratch_shapes=list(scratch),
        compiler_params=pltpu.CompilerParams(vmem_limit_bytes=limit << 20),
        name=name,
    )


def like(shape, dtype):
    return jax.ShapeDtypeStruct(shape, dtype)


def own_sector():
    return lax.axis_index("sec")


def row_index(shape, base=0):
    return base + lax.broadcasted_iota(jnp.int32, shape, len(shape) - 2)


def begin_body(block_rows_ref, guess_ref, out_ref):
    live = row_index(guess_ref.shape) < block_rows_ref[own_sector()]
    out_ref[...] = jnp.where(live, guess_ref[...], 0.0).astype(out_ref.dtype)


def begin(block_rows, guess):
    return call(begin_body, "begin", like(guess.shape, jnp.bfloat16), [SMEM, VMEM])(
        block_rows, guess
    )


def terms_body(
    block_rows_ref, charges_ref, own_ref, partner_ref, other_ref, ahead_ref, behind_ref,
    left_ref, right_ref, out_ref, held, middles,
):
    sector = own_sector()
    sectors = block_rows_ref.shape[0]
    core = lax.rem(sector, 2)
    held[0] = ahead_ref[...]
    held[2] = own_ref[...]
    held[4] = behind_ref[...]
    held[1 + 2 * core] = partner_ref[...]
    held[3 - 2 * core] = other_ref[...]
    own_rows = block_rows_ref[sector]
    terms, capacity, _ = left_ref.shape
    tiles = capacity // TILE

    def apply_term(term, _):
        charge = charges_ref[term]
        source_rows = block_rows_ref[lax.rem(sector - charge + sectors, sectors)]
        for i in range(1, tiles + 1):
            for j in range(1, tiles + 1):
                fits = (own_rows > (i - 1) * TILE) & (source_rows > (j - 1) * TILE)
                if i < tiles:
                    fits = fits & (own_rows <= i * TILE)
                if j < tiles:
                    fits = fits & (source_rows <= j * TILE)

                @pl.when(fits)
                def _():
                    middles[term, : i * TILE, :] = jnp.dot(
                        left_ref[term, : i * TILE, : j * TILE],
                        held[REACH + charge, : j * TILE, :],
                        preferred_element_type=jnp.float32,
                    ).astype(jnp.bfloat16)
        return 0

    lax.fori_loop(0, terms, apply_term, 0)
    for i in range(1, tiles + 1):
        fits = own_rows > (i - 1) * TILE
        if i < tiles:
            fits = fits & (own_rows <= i * TILE)

        @pl.when(fits)
        def _():
            high = i * TILE
            total = 0.0
            for term in range(terms):
                total = total + jnp.dot(
                    middles[term, :high, :], right_ref[term], preferred_element_type=jnp.float32
                )
            live = row_index(total.shape) < own_rows
            out_ref[:high, :] = jnp.where(live, total, 0.0).astype(out_ref.dtype)
            if high < capacity:
                out_ref[high:, :] = jnp.zeros((capacity - high, total.shape[1]), out_ref.dtype)


def apply_terms(block_rows, charges, blocks, left_env, right_env):
    terms, capacity, _ = left_env.shape
    width = right_env.shape[-1]
    return call(
        terms_body,
        "apply_terms",
        like((capacity, width), jnp.bfloat16),
        [SMEM, SMEM] + [VMEM] * 7,
        [
            pltpu.VMEM((2 * REACH + 1, capacity, width), jnp.bfloat16),
            pltpu.VMEM((terms, capacity, width), jnp.bfloat16),
        ],
    )(block_rows, charges, *blocks, left_env, right_env)


def next_slab(pieces_ref, slab):
    applied = jnp.sum(pieces_ref[...].astype(jnp.float32), axis=0)
    return (slab - step_size * applied) * SHRINK


def first_slab_body(block_rows_ref, guess_ref, pieces_ref, start_ref, new_ref, sent_ref):
    rows = start_ref.shape[0]
    base = pl.multiple_of(lax.axis_index("mpo") * rows, 8)
    slab = guess_ref[pl.ds(base, rows), :]
    slab = jnp.where(row_index(slab.shape, base) < block_rows_ref[own_sector()], slab, 0.0)
    start_ref[...] = slab
    new = next_slab(pieces_ref, slab)
    new_ref[...] = new
    sent_ref[...] = jnp.broadcast_to(new.astype(sent_ref.dtype)[None], sent_ref.shape)


def slab_body(slab_ref, pieces_ref, new_ref, sent_ref):
    new = next_slab(pieces_ref, slab_ref[...])
    new_ref[...] = new
    sent_ref[...] = jnp.broadcast_to(new.astype(sent_ref.dtype)[None], sent_ref.shape)


def last_slab_body(*refs):
    slab_refs, (pieces_ref, new_ref, sent_ref) = refs[:ITERS], refs[ITERS:]
    slabs = [ref[...] for ref in slab_refs]
    new = next_slab(pieces_ref, slabs[-1])
    new_ref[...] = new
    slabs.append(new)
    members, rows, width = pieces_ref.shape
    lane = lax.broadcasted_iota(jnp.int32, (1, width), 1)
    table = jnp.zeros((1, width), jnp.float32)
    for place, (i, j) in enumerate(PAIRS):
        value = jnp.sum(jnp.sum(slabs[i] * slabs[j], axis=0, keepdims=True), axis=1, keepdims=True)
        table = table + jnp.where(lane == place, value, 0.0)
    high = table.astype(jnp.bfloat16)
    rest = table - high.astype(jnp.float32)
    middle = rest.astype(jnp.bfloat16)
    low = (rest - middle.astype(jnp.float32)).astype(jnp.bfloat16)
    row = row_index((EXTRA, width))
    packed = jnp.where(
        row == 0,
        high.astype(jnp.float32),
        jnp.where(
            row == 1,
            middle.astype(jnp.float32),
            jnp.where(row == 2, low.astype(jnp.float32), 0.0),
        ),
    ).astype(jnp.bfloat16)
    sent_ref[:, :rows, :] = jnp.broadcast_to(new.astype(jnp.bfloat16)[None], pieces_ref.shape)
    sent_ref[:, rows:, :] = jnp.broadcast_to(packed[None], (members, EXTRA, width))


def table_body(gathered_ref, out_ref):
    rows = gathered_ref.shape[1] - EXTRA
    parts = gathered_ref[:, rows:, :].astype(jnp.float32)
    summed = jnp.sum(jnp.sum(parts, axis=0), axis=0, keepdims=True)
    out_ref[...] = jnp.broadcast_to(summed[None, :, :128], out_ref.shape)


def dot32(a, b, dims):
    return lax.dot_general(
        a, b, (dims, ((), ())), precision=highest, preferred_element_type=jnp.float32
    )


def inverse_of(block):
    size = block.shape[0]
    row = lax.broadcasted_iota(jnp.int32, block.shape, 0)
    lane = lax.broadcasted_iota(jnp.int32, block.shape, 1)
    for k in range(0, size, 2):
        row0, row1 = block[k : k + 1, :], block[k + 1 : k + 2, :]
        col0 = jnp.broadcast_to(block[:, k : k + 1], block.shape)
        col1 = jnp.broadcast_to(block[:, k + 1 : k + 2], block.shape)
        a, b, d = col0[k : k + 1, :], col0[k + 1 : k + 2, :], col1[k + 1 : k + 2, :]
        scale = 1.0 / (a * d - b * b)
        at0, at1 = lane[:1] == k, lane[:1] == k + 1
        row0 = jnp.where(at0, -1.0, jnp.where(at1, 0.0, row0))
        row1 = jnp.where(at1, -1.0, jnp.where(at0, 0.0, row1))
        new0 = (d * scale) * row0 - (b * scale) * row1
        new1 = (a * scale) * row1 - (b * scale) * row0
        rest = jnp.where((lane == k) | (lane == k + 1), 0.0, block) - col0 * new0 - col1 * new1
        block = jnp.where(row == k, new0, jnp.where(row == k + 1, new1, rest))
    return -block


def weights_of(sums_ref):
    sectors = sums_ref.shape[0]
    summed = jnp.sum(sums_ref[...], axis=0)
    table = {}
    for place, (i, j) in enumerate(PAIRS):
        table[i, j] = table[j, i] = summed[:, place : place + 1]

    def inner(a, b):
        out = 0.0
        for i, x in enumerate(a):
            for j, y in enumerate(b):
                out = out + x * y * table[i, j]
        return out

    entries = float(MEAN * sectors * 256)

    def scale_of(squares):
        return lax.rsqrt(squares / entries + epsilon)

    weights = [scale_of(table[0, 0])]
    for _ in range(ITERS):
        up = [0.0 * weights[0]] + [x * (1.0 / SHRINK) for x in weights]
        padded = weights + [0.0 * weights[0]]
        image = [(x - y) * (1.0 / step_size) for x, y in zip(padded, up)]
        rayleigh = inner(weights, image) / (inner(weights, weights) + epsilon)
        update = [y + step_size * rayleigh * x for x, y in zip(padded, up)]
        scale = scale_of(jnp.maximum(inner(update, update), 0.0))
        weights = [x * scale for x in update]
    return weights


def truncate_body(block_rows_ref, ranks_ref, sums_ref, guess_ref, *refs):
    powers = refs[:ITERS]
    slabs = refs[ITERS : 2 * ITERS + 1]
    slab_ref, cut_ref, gram = refs[2 * ITERS + 1 :]
    sector = own_sector()
    weights = weights_of(sums_ref)
    slab_rows, width = slab_ref.shape
    live = row_index(guess_ref.shape) < block_rows_ref[sector]
    current = jnp.where(live, guess_ref[...], 0.0) * weights[0]
    for weight, ref in zip(weights[1:], powers):
        power = ref[...] if len(ref.shape) == 2 else ref[:, :slab_rows, :].reshape(current.shape)
        current = current + weight * power.astype(jnp.float32)
    density = dot32(current, current, ((0,), (0,)))
    row = lax.broadcasted_iota(jnp.int32, density.shape, 0)
    lane = lax.broadcasted_iota(jnp.int32, density.shape, 1)
    diagonal = (row == lane).astype(jnp.float32)
    kept = lane < ranks_ref[sector]
    basis = jnp.where(kept, diagonal + density * (1.0 / MEAN), 0.0)
    gram[...] = dot32(basis, basis, ((0,), (0,))) + jnp.where(kept, 0.0, diagonal)
    panel_row = lax.broadcasted_iota(jnp.int32, (BASE, width), 0)
    panel_lane = lax.broadcasted_iota(jnp.int32, (BASE, width), 1)
    for low in range(0, width, BASE):
        panel = gram[low : low + BASE, :]
        inverse = inverse_of(panel[:, low : low + BASE])
        inside = (panel_lane >= low) & (panel_lane < low + BASE)
        select = (panel_lane == panel_row + low).astype(jnp.float32)
        rest = jnp.where(inside, 0.0, panel)
        solved = dot32(inverse, rest, ((1,), (0,)))
        change = dot32(
            jnp.concatenate([rest, solved], axis=0),
            jnp.concatenate([solved, -select], axis=0),
            ((0,), (0,)),
        )
        taken = (lane >= low) & (lane < low + BASE)
        gram[...] = jnp.where(taken, 0.0, gram[...]) - change
        gram[low : low + BASE, :] = solved - dot32(inverse, select, ((1,), (0,)))
    slab = weights[0] * slabs[0][...]
    for weight, ref in zip(weights[1:], slabs[1:]):
        slab = slab + weight * ref[...]
    slab_ref[...] = slab
    coords = dot32(slab, basis, ((1,), (0,)))
    solved = -dot32(coords, gram[...], ((1,), (0,)))
    cut_ref[...] = dot32(solved, basis, ((1,), (1,)))


def passed_along(array, by):
    peers = lax.axis_size("sec")
    return lax.ppermute(array, "sec", [(i, (i + by) % peers) for i in range(peers)])


def swapped(array):
    peers = lax.axis_size("sec")
    return lax.ppermute(array, "sec", [(i, i ^ 1) for i in range(peers)])


def neighbours(whole):
    ahead, behind = passed_along(whole, -2), passed_along(whole, 2)
    whole, ahead, behind = lax.optimization_barrier((whole, ahead, behind))
    partner = swapped(whole)
    other = swapped(jnp.where(own_sector() % 2 == 0, ahead, behind))
    return whole, partner, other, ahead, behind


def shards(guess, left_env, right_env, block_rows, charges, ranks):
    capacity, width = guess.shape
    sectors = block_rows.shape[0]
    members = lax.axis_size("mpo")
    rows = capacity // members
    exact = like((rows, width), jnp.float32)
    sent = like((members, rows, width), jnp.bfloat16)
    sent_last = like((members, rows + EXTRA, width), jnp.bfloat16)

    def exchanged(array, axis):
        return lax.all_to_all(array, axis, 0, 0, tiled=True)

    whole = begin(block_rows, guess)
    powers, slabs = [], []
    for repeat in range(ITERS):
        part = apply_terms(block_rows, charges, neighbours(whole), left_env, right_env)
        pieces = exchanged(part.reshape(members, rows, width), "mpo")
        if repeat == 0:
            start, new, outgoing = call(
                first_slab_body, "first_slab", (exact, exact, sent), [SMEM, VMEM, VMEM]
            )(block_rows, guess, pieces)
            slabs.append(start)
        elif repeat < ITERS - 1:
            new, outgoing = call(slab_body, "slab", (exact, sent), [VMEM] * 2)(slabs[-1], pieces)
        else:
            new, outgoing = call(
                last_slab_body, "last_slab", (exact, sent_last), [VMEM] * (ITERS + 1)
            )(*slabs, pieces)
        slabs.append(new)
        gathered = exchanged(outgoing, "mpo")
        whole = gathered.reshape(capacity, width) if repeat < ITERS - 1 else gathered
        powers.append(whole)
    tables = call(table_body, "table", like((sectors, 1, 128), jnp.float32), [VMEM])(powers[-1])
    sums = exchanged(tables, "sec")
    return call(
        truncate_body,
        "truncate",
        (exact, exact),
        [SMEM, SMEM] + [VMEM] * (3 + 2 * ITERS),
        [pltpu.VMEM((width, width), jnp.float32)],
        limit=24,
    )(block_rows, ranks, sums, guess, *powers, *slabs)


def solution(mesh):
    return jax.shard_map(
        shards,
        mesh=mesh,
        in_specs=(P("sec", None), P("mpo", "sec", None), P("mpo", "sec", None), P(), P("mpo"), P()),
        out_specs=(P(("sec", "mpo"), None), P(("sec", "mpo"), None)),
        check_vma=False,
    )
```

```python
import jax
import jax.numpy as jnp
from jax import lax
from jax.experimental import pallas as pl
from jax.experimental.pallas import tpu as pltpu
from jax.sharding import PartitionSpec as P

MEAN = 256
ITERS = 4
REACH = 2
SHRINK = 2.0**-4
epsilon = 1e-06
step_size = 0.1
highest = lax.Precision.HIGHEST
TILE = 256
BASE = 128
PAIRS = [(i, j) for i in range(ITERS + 1) for j in range(i, ITERS + 1)]
SMEM = pl.BlockSpec(memory_space=pltpu.SMEM)
VMEM = pl.BlockSpec(memory_space=pltpu.VMEM)


def call(body, name, out_shape, in_specs, scratch=(), limit=16):
    return pl.pallas_call(
        body,
        in_specs=in_specs,
        out_specs=jax.tree.map(lambda _: VMEM, out_shape),
        out_shape=out_shape,
        scratch_shapes=list(scratch),
        compiler_params=pltpu.CompilerParams(vmem_limit_bytes=limit << 20),
        name=name,
    )


def like(shape, dtype):
    return jax.ShapeDtypeStruct(shape, dtype)


def own_sector():
    return lax.axis_index("sec")


def row_index(shape, base=0):
    return base + lax.broadcasted_iota(jnp.int32, shape, len(shape) - 2)


def begin_body(block_rows_ref, guess_ref, out_ref):
    live = row_index(guess_ref.shape) < block_rows_ref[own_sector()]
    out_ref[...] = jnp.where(live, guess_ref[...], 0.0).astype(out_ref.dtype)


def begin(block_rows, guess):
    return call(begin_body, "begin", like(guess.shape, jnp.bfloat16), [SMEM, VMEM])(
        block_rows, guess
    )


def tile_cases(rows, tiles):
    cases = []
    for i in range(1, tiles + 1):
        fits = rows > (i - 1) * TILE
        cases.append((i * TILE, fits if i == tiles else fits & (rows <= i * TILE)))
    return cases


def middle_of(left, block):
    return jnp.dot(left, block, preferred_element_type=jnp.float32).astype(jnp.bfloat16)


def own_term_body(block_rows_ref, charges_ref, own_ref, left_ref, right_ref, out_ref):
    terms, capacity, _ = left_ref.shape

    def apply_term(term, _):
        for high, fits in tile_cases(block_rows_ref[own_sector()], capacity // TILE):

            @pl.when(fits & (charges_ref[term] == 0))
            def _():
                out_ref[:high, :] = middle_of(left_ref[term, :high, :high], own_ref[:high, :])
        return 0

    lax.fori_loop(0, terms, apply_term, 0)


def terms_body(
    block_rows_ref, charges_ref, done_ref, partner_ref, other_ref, ahead_ref, behind_ref,
    left_ref, right_ref, out_ref, held, middles,
):
    sector = own_sector()
    sectors = block_rows_ref.shape[0]
    core = lax.rem(sector, 2)
    held[0] = ahead_ref[...]
    held[4] = behind_ref[...]
    held[1 + 2 * core] = partner_ref[...]
    held[3 - 2 * core] = other_ref[...]
    terms, capacity, _ = left_ref.shape
    tiles = capacity // TILE
    own_cases = tile_cases(block_rows_ref[sector], tiles)

    def apply_term(term, _):
        charge = charges_ref[term]
        source_rows = block_rows_ref[lax.rem(sector - charge + sectors, sectors)]

        @pl.when(charge == 0)
        def _():
            middles[term] = done_ref[...]

        for high, own_fits in own_cases:
            for wide, source_fits in tile_cases(source_rows, tiles):

                @pl.when(own_fits & source_fits & (charge != 0))
                def _():
                    middles[term, :high, :] = middle_of(
                        left_ref[term, :high, :wide], held[REACH + charge, :wide, :]
                    )
        return 0

    lax.fori_loop(0, terms, apply_term, 0)
    for high, fits in own_cases:

        @pl.when(fits)
        def _():
            total = 0.0
            for term in range(terms):
                total = total + jnp.dot(
                    middles[term, :high, :], right_ref[term], preferred_element_type=jnp.float32
                )
            live = row_index(total.shape) < block_rows_ref[sector]
            out_ref[:high, :] = jnp.where(live, total, 0.0).astype(out_ref.dtype)
            if high < capacity:
                out_ref[high:, :] = jnp.zeros((capacity - high, total.shape[1]), out_ref.dtype)


def apply_terms(block_rows, charges, whole, left_env, right_env):
    terms, capacity, _ = left_env.shape
    width = right_env.shape[-1]
    block = like((capacity, width), jnp.bfloat16)
    done = call(own_term_body, "own_term", block, [SMEM, SMEM] + [VMEM] * 3)(
        block_rows, charges, whole, left_env, right_env
    )
    return call(
        terms_body,
        "apply_terms",
        block,
        [SMEM, SMEM] + [VMEM] * 7,
        [
            pltpu.VMEM((2 * REACH + 1, capacity, width), jnp.bfloat16),
            pltpu.VMEM((terms, capacity, width), jnp.bfloat16),
        ],
    )(block_rows, charges, *neighbours(whole, done), left_env, right_env)


def next_slab(pieces_ref, slab):
    applied = jnp.sum(pieces_ref[...].astype(jnp.float32), axis=0)
    return (slab - step_size * applied) * SHRINK


def first_slab_body(block_rows_ref, guess_ref, pieces_ref, start_ref, new_ref, sent_ref):
    rows = start_ref.shape[0]
    base = pl.multiple_of(lax.axis_index("mpo") * rows, 8)
    slab = guess_ref[pl.ds(base, rows), :]
    slab = jnp.where(row_index(slab.shape, base) < block_rows_ref[own_sector()], slab, 0.0)
    start_ref[...] = slab
    new = next_slab(pieces_ref, slab)
    new_ref[...] = new
    sent_ref[...] = jnp.broadcast_to(new.astype(sent_ref.dtype)[None], sent_ref.shape)


def slab_body(slab_ref, pieces_ref, new_ref, sent_ref):
    new = next_slab(pieces_ref, slab_ref[...])
    new_ref[...] = new
    sent_ref[...] = jnp.broadcast_to(new.astype(sent_ref.dtype)[None], sent_ref.shape)


def last_slab_body(*refs):
    slab_refs, (pieces_ref, new_ref, sent_ref, table_ref) = refs[:ITERS], refs[ITERS:]
    slabs = [ref[...] for ref in slab_refs]
    new = next_slab(pieces_ref, slabs[-1])
    new_ref[...] = new
    sent_ref[...] = new.astype(sent_ref.dtype)
    slabs.append(new)
    lane = lax.broadcasted_iota(jnp.int32, (1, 128), 1)
    table = jnp.zeros((1, 128), jnp.float32)
    for place, (i, j) in enumerate(PAIRS):
        value = jnp.sum(jnp.sum(slabs[i] * slabs[j], axis=0, keepdims=True), axis=1, keepdims=True)
        table = table + jnp.where(lane == place, value, 0.0)
    table_ref[...] = jnp.broadcast_to(table[None], table_ref.shape)


def fold_body(tables_ref, out_ref):
    out_ref[...] = jnp.broadcast_to(
        jnp.sum(tables_ref[...], axis=0, keepdims=True), out_ref.shape
    )


def dot32(a, b, dims):
    return lax.dot_general(
        a, b, (dims, ((), ())), precision=highest, preferred_element_type=jnp.float32
    )


def inverse_of(block):
    size = block.shape[0]
    row = lax.broadcasted_iota(jnp.int32, block.shape, 0)
    lane = lax.broadcasted_iota(jnp.int32, block.shape, 1)
    for k in range(0, size, 4):
        cols = [jnp.broadcast_to(block[:, k + i : k + i + 1], block.shape) for i in range(4)]
        pivot = {(i, j): cols[j][k + i : k + i + 1, :] for i in range(4) for j in range(4)}
        rows = []
        for i in range(4):
            new = block[k + i : k + i + 1, :]
            for j in range(4):
                new = jnp.where(lane[:1] == k + j, -1.0 if i == j else 0.0, new)
            rows.append(new)
        a0, a1, a2 = pivot[0, 0], pivot[1, 0], pivot[1, 1]
        scale = 1.0 / (a0 * a2 - a1 * a1)
        a0, a1, a2 = a2 * scale, -a1 * scale, a0 * scale
        b00, b01, b10, b11 = pivot[2, 0], pivot[3, 0], pivot[2, 1], pivot[3, 1]
        x00, x01 = a0 * b00 + a1 * b10, a0 * b01 + a1 * b11
        x10, x11 = a1 * b00 + a2 * b10, a1 * b01 + a2 * b11
        s0 = pivot[2, 2] - (b00 * x00 + b10 * x10)
        s1 = pivot[3, 2] - (b00 * x01 + b10 * x11)
        s2 = pivot[3, 3] - (b01 * x01 + b11 * x11)
        scale = 1.0 / (s0 * s2 - s1 * s1)
        s0, s1, s2 = s2 * scale, -s1 * scale, s0 * scale
        low0 = rows[2] - (x00 * rows[0] + x10 * rows[1])
        low1 = rows[3] - (x01 * rows[0] + x11 * rows[1])
        new2, new3 = s0 * low0 + s1 * low1, s1 * low0 + s2 * low1
        new0 = (a0 * rows[0] + a1 * rows[1]) - (x00 * new2 + x01 * new3)
        new1 = (a1 * rows[0] + a2 * rows[1]) - (x10 * new2 + x11 * new3)
        block = jnp.where((lane >= k) & (lane < k + 4), 0.0, block)
        block = (block - (cols[0] * new0 + cols[1] * new1)) - (cols[2] * new2 + cols[3] * new3)
        for i, new in enumerate((new0, new1, new2, new3)):
            block = jnp.where(row == k + i, new, block)
    return -block


def weights_of(sums_ref, entries):
    summed = jnp.sum(sums_ref[...], axis=0)
    table = {}
    for place, (i, j) in enumerate(PAIRS):
        table[i, j] = table[j, i] = summed[:, place : place + 1]

    def inner(a, b):
        out = 0.0
        for i, x in enumerate(a):
            for j, y in enumerate(b):
                out = out + x * y * table[i, j]
        return out

    def scale_of(squares):
        return lax.rsqrt(squares / entries + epsilon)

    weights = [scale_of(table[0, 0])]
    for _ in range(ITERS):
        up = [0.0 * weights[0]] + [x * (1.0 / SHRINK) for x in weights]
        padded = weights + [0.0 * weights[0]]
        image = [(x - y) * (1.0 / step_size) for x, y in zip(padded, up)]
        rayleigh = inner(weights, image) / (inner(weights, weights) + epsilon)
        update = [y + step_size * rayleigh * x for x, y in zip(padded, up)]
        scale = scale_of(jnp.maximum(inner(update, update), 0.0))
        weights = [x * scale for x in update]
    return weights


def truncate_body(block_rows_ref, ranks_ref, sums_ref, guess_ref, *refs):
    powers = refs[: ITERS - 1]
    last = refs[ITERS - 1 : ITERS + 4]
    slabs = refs[ITERS + 4 : 2 * ITERS + 5]
    slab_ref, cut_ref, state, gram = refs[2 * ITERS + 5 :]
    sector = own_sector()
    slab_rows, width = slab_ref.shape
    capacity = guess_ref.shape[0]
    members = capacity // slab_rows
    weights = weights_of(sums_ref, float(MEAN * block_rows_ref.shape[0] * width))
    live = row_index(guess_ref.shape) < block_rows_ref[sector]
    current = jnp.where(live, guess_ref[...], 0.0) * weights[0]
    for weight, ref in zip(weights[1:], powers):
        current = current + weight * ref[...].astype(jnp.float32)
    state[...] = current
    member = lax.axis_index("mpo")
    own, before, after, far_before, far_after = last
    pieces = [(own, 0), (before, -1), (after, 1)]
    pieces += [(far_before.at[i], -4 + i) for i in range(3)]
    pieces += [(far_after.at[i], 2 + i) for i in range(2)]
    for piece, by in pieces:
        place = lax.rem(member + by + members, members)
        span = pl.ds(pl.multiple_of(place * slab_rows, 8), slab_rows)
        state[span, :] += weights[-1] * piece[...].astype(jnp.float32)
    current = state[...]
    density = dot32(current, current, ((0,), (0,)))
    row = lax.broadcasted_iota(jnp.int32, density.shape, 0)
    lane = lax.broadcasted_iota(jnp.int32, density.shape, 1)
    diagonal = (row == lane).astype(jnp.float32)
    kept = lane < ranks_ref[sector]
    basis = jnp.where(kept, diagonal + density * (1.0 / MEAN), 0.0)
    gram[...] = dot32(basis, basis, ((0,), (0,))) + jnp.where(kept, 0.0, diagonal)
    panel_row = lax.broadcasted_iota(jnp.int32, (BASE, width), 0)
    panel_lane = lax.broadcasted_iota(jnp.int32, (BASE, width), 1)
    for low in range(0, width, BASE):
        panel = gram[low : low + BASE, :]
        inverse = inverse_of(panel[:, low : low + BASE])
        inside = (panel_lane >= low) & (panel_lane < low + BASE)
        select = (panel_lane == panel_row + low).astype(jnp.float32)
        rest = jnp.where(inside, 0.0, panel)
        solved = dot32(inverse, rest, ((1,), (0,)))
        change = dot32(
            jnp.concatenate([rest, solved], axis=0),
            jnp.concatenate([solved, -select], axis=0),
            ((0,), (0,)),
        )
        taken = (lane >= low) & (lane < low + BASE)
        gram[...] = jnp.where(taken, 0.0, gram[...]) - change
        gram[low : low + BASE, :] = solved - dot32(inverse, select, ((1,), (0,)))
    slab = weights[0] * slabs[0][...]
    for weight, ref in zip(weights[1:], slabs[1:]):
        slab = slab + weight * ref[...]
    slab_ref[...] = slab
    coords = dot32(slab, basis, ((1,), (0,)))
    solved = -dot32(coords, gram[...], ((1,), (0,)))
    cut_ref[...] = dot32(solved, basis, ((1,), (1,)))


def passed_along(array, by):
    peers = lax.axis_size("sec")
    return lax.ppermute(array, "sec", [(i, (i + by) % peers) for i in range(peers)])


def swapped(array):
    peers = lax.axis_size("sec")
    return lax.ppermute(array, "sec", [(i, i ^ 1) for i in range(peers)])


def neighbours(whole, done):
    ahead, behind = passed_along(whole, -2), passed_along(whole, 2)
    whole, done, ahead, behind = lax.optimization_barrier((whole, done, ahead, behind))
    partner = swapped(whole)
    other = swapped(jnp.where(own_sector() % 2 == 0, ahead, behind))
    return done, partner, other, ahead, behind


def shards(guess, left_env, right_env, block_rows, charges, ranks):
    capacity, width = guess.shape
    sectors = block_rows.shape[0]
    members = lax.axis_size("mpo")
    rows = capacity // members
    exact = like((rows, width), jnp.float32)
    sent = like((members, rows, width), jnp.bfloat16)

    def exchanged(array, axis):
        return lax.all_to_all(array, axis, 0, 0, tiled=True)

    def along(array, by):
        return lax.ppermute(array, "mpo", [(i, (i + by) % members) for i in range(members)])

    whole = begin(block_rows, guess)
    powers, slabs = [], []
    for repeat in range(ITERS - 1):
        part = apply_terms(block_rows, charges, whole, left_env, right_env)
        pieces = exchanged(part.reshape(members, rows, width), "mpo")
        if repeat == 0:
            start, new, outgoing = call(
                first_slab_body, "first_slab", (exact, exact, sent), [SMEM, VMEM, VMEM]
            )(block_rows, guess, pieces)
            slabs.append(start)
        else:
            new, outgoing = call(slab_body, "slab", (exact, sent), [VMEM] * 2)(slabs[-1], pieces)
        slabs.append(new)
        whole = exchanged(outgoing, "mpo").reshape(capacity, width)
        powers.append(whole)
    part = apply_terms(block_rows, charges, whole, left_env, right_env)
    pieces = exchanged(part.reshape(members, rows, width), "mpo")
    new, own, tables = call(
        last_slab_body,
        "last_slab",
        (exact, like((rows, width), jnp.bfloat16), like((sectors, 1, 128), jnp.float32)),
        [VMEM] * (ITERS + 1),
    )(*slabs, pieces)
    slabs.append(new)
    before, after = along(own, 1), along(own, -1)
    before, after, sums = lax.optimization_barrier((before, after, exchanged(tables, "sec")))
    far_before = along(jnp.stack([before, own, after]), 3)
    far_after = along(jnp.stack([before, own]), -3)
    sums = call(fold_body, "fold", like((members, 1, 128), jnp.float32), [VMEM])(sums)
    sums = exchanged(sums, "mpo")
    return call(
        truncate_body,
        "truncate",
        (exact, exact),
        [SMEM, SMEM] + [VMEM] * (2 * ITERS + 7),
        [pltpu.VMEM((capacity, width), jnp.float32), pltpu.VMEM((width, width), jnp.float32)],
        limit=24,
    )(block_rows, ranks, sums, guess, *powers, own, before, after, far_before, far_after, *slabs)


def solution(mesh):
    return jax.shard_map(
        shards,
        mesh=mesh,
        in_specs=(P("sec", None), P("mpo", "sec", None), P("mpo", "sec", None), P(), P("mpo"), P()),
        out_specs=(P(("sec", "mpo"), None), P(("sec", "mpo"), None)),
        check_vma=False,
    )
```

```python
import jax
import jax.numpy as jnp
from jax import lax
from jax.experimental import pallas as pl
from jax.experimental.pallas import tpu as pltpu
from jax.sharding import PartitionSpec as P

MEAN = 256
ITERS = 4
REACH = 2
SHRINK = 2.0**-4
epsilon = 1e-06
step_size = 0.1
highest = lax.Precision.HIGHEST
TILE = 256
BASE = 64
PAIRS = [(i, j) for i in range(ITERS + 1) for j in range(i, ITERS + 1)]
SMEM = pl.BlockSpec(memory_space=pltpu.SMEM)
VMEM = pl.BlockSpec(memory_space=pltpu.VMEM)


def call(body, name, out_shape, in_specs, scratch=(), limit=16):
    return pl.pallas_call(
        body,
        in_specs=in_specs,
        out_specs=jax.tree.map(lambda _: VMEM, out_shape),
        out_shape=out_shape,
        scratch_shapes=list(scratch),
        compiler_params=pltpu.CompilerParams(vmem_limit_bytes=limit << 20),
        name=name,
    )


def like(shape, dtype):
    return jax.ShapeDtypeStruct(shape, dtype)


def own_sector():
    return lax.axis_index("sec")


def row_index(shape, base=0):
    return base + lax.broadcasted_iota(jnp.int32, shape, len(shape) - 2)


def begin_body(block_rows_ref, guess_ref, out_ref):
    live = row_index(guess_ref.shape) < block_rows_ref[own_sector()]
    out_ref[...] = jnp.where(live, guess_ref[...], 0.0).astype(out_ref.dtype)


def begin(block_rows, guess):
    return call(begin_body, "begin", like(guess.shape, jnp.bfloat16), [SMEM, VMEM])(
        block_rows, guess
    )


def tile_cases(rows, tiles):
    cases = []
    for i in range(1, tiles + 1):
        fits = rows > (i - 1) * TILE
        cases.append((i * TILE, fits if i == tiles else fits & (rows <= i * TILE)))
    return cases


def middle_of(left, block):
    return jnp.dot(left, block, preferred_element_type=jnp.float32).astype(jnp.bfloat16)


def own_term_body(block_rows_ref, charges_ref, own_ref, left_ref, right_ref, out_ref):
    terms, capacity, _ = left_ref.shape

    def apply_term(term, _):
        for high, fits in tile_cases(block_rows_ref[own_sector()], capacity // TILE):

            @pl.when(fits & (charges_ref[term] == 0))
            def _():
                out_ref[:high, :] = middle_of(left_ref[term, :high, :high], own_ref[:high, :])
        return 0

    lax.fori_loop(0, terms, apply_term, 0)


def terms_body(
    block_rows_ref, charges_ref, done_ref, partner_ref, before_ref, after_ref, ahead_ref, behind_ref,
    left_ref, right_ref, out_ref, held, middles,
):
    sector = own_sector()
    sectors = block_rows_ref.shape[0]
    core = lax.rem(sector, 2)
    held[0] = ahead_ref[...]
    held[4] = behind_ref[...]

    @pl.when(core == 0)
    def _():
        held[1] = partner_ref[...]
        held[3] = before_ref[...]

    @pl.when(core == 1)
    def _():
        held[1] = after_ref[...]
        held[3] = partner_ref[...]

    terms, capacity, _ = left_ref.shape
    tiles = capacity // TILE
    own_cases = tile_cases(block_rows_ref[sector], tiles)

    def apply_term(term, _):
        charge = charges_ref[term]
        source_rows = block_rows_ref[lax.rem(sector - charge + sectors, sectors)]

        @pl.when(charge == 0)
        def _():
            middles[term] = done_ref[...]

        for high, own_fits in own_cases:
            for wide, source_fits in tile_cases(source_rows, tiles):

                @pl.when(own_fits & source_fits & (charge != 0))
                def _():
                    middles[term, :high, :] = middle_of(
                        left_ref[term, :high, :wide], held[REACH + charge, :wide, :]
                    )
        return 0

    lax.fori_loop(0, terms, apply_term, 0)
    for high, fits in own_cases:

        @pl.when(fits)
        def _():
            total = 0.0
            for term in range(terms):
                total = total + jnp.dot(
                    middles[term, :high, :], right_ref[term], preferred_element_type=jnp.float32
                )
            live = row_index(total.shape) < block_rows_ref[sector]
            out_ref[:high, :] = jnp.where(live, total, 0.0).astype(out_ref.dtype)
            if high < capacity:
                out_ref[high:, :] = jnp.zeros((capacity - high, total.shape[1]), out_ref.dtype)


def apply_terms(block_rows, charges, whole, left_env, right_env):
    terms, capacity, _ = left_env.shape
    width = right_env.shape[-1]
    block = like((capacity, width), jnp.bfloat16)
    done = call(own_term_body, "own_term", block, [SMEM, SMEM] + [VMEM] * 3)(
        block_rows, charges, whole, left_env, right_env
    )
    return call(
        terms_body,
        "apply_terms",
        block,
        [SMEM, SMEM] + [VMEM] * 8,
        [
            pltpu.VMEM((2 * REACH + 1, capacity, width), jnp.bfloat16),
            pltpu.VMEM((terms, capacity, width), jnp.bfloat16),
        ],
    )(block_rows, charges, *neighbours(whole, done), left_env, right_env)


def next_slab(pieces_ref, slab):
    applied = jnp.sum(pieces_ref[...].astype(jnp.float32), axis=0)
    return (slab - step_size * applied) * SHRINK


def first_slab_body(block_rows_ref, guess_ref, pieces_ref, start_ref, new_ref, sent_ref):
    rows = start_ref.shape[0]
    base = pl.multiple_of(lax.axis_index("mpo") * rows, 8)
    slab = guess_ref[pl.ds(base, rows), :]
    slab = jnp.where(row_index(slab.shape, base) < block_rows_ref[own_sector()], slab, 0.0)
    start_ref[...] = slab
    new = next_slab(pieces_ref, slab)
    new_ref[...] = new
    sent_ref[...] = jnp.broadcast_to(new.astype(sent_ref.dtype)[None], sent_ref.shape)


def slab_body(slab_ref, pieces_ref, new_ref, sent_ref):
    new = next_slab(pieces_ref, slab_ref[...])
    new_ref[...] = new
    sent_ref[...] = jnp.broadcast_to(new.astype(sent_ref.dtype)[None], sent_ref.shape)


def last_slab_body(*refs):
    slab_refs, (pieces_ref, new_ref, sent_ref, table_ref) = refs[:ITERS], refs[ITERS:]
    slabs = [ref[...] for ref in slab_refs]
    new = next_slab(pieces_ref, slabs[-1])
    new_ref[...] = new
    sent_ref[...] = new.astype(sent_ref.dtype)
    slabs.append(new)
    lane = lax.broadcasted_iota(jnp.int32, (1, 128), 1)
    table = jnp.zeros((1, 128), jnp.float32)
    for place, (i, j) in enumerate(PAIRS):
        value = jnp.sum(jnp.sum(slabs[i] * slabs[j], axis=0, keepdims=True), axis=1, keepdims=True)
        table = table + jnp.where(lane == place, value, 0.0)
    table_ref[...] = jnp.broadcast_to(table[None], table_ref.shape)


def fold_body(tables_ref, out_ref):
    out_ref[...] = jnp.broadcast_to(
        jnp.sum(tables_ref[...], axis=0, keepdims=True), out_ref.shape
    )


def dot32(a, b, dims):
    return lax.dot_general(
        a, b, (dims, ((), ())), precision=highest, preferred_element_type=jnp.float32
    )


def inverse_of(block):
    size = block.shape[0]
    lane = lax.broadcasted_iota(jnp.int32, block.shape, 1)
    row8 = lax.broadcasted_iota(jnp.int32, (8, size), 0)
    lane8 = lane[:8]
    for k in range(0, size, 8):
        cols = [jnp.broadcast_to(block[:, k + i : k + i + 1], block.shape) for i in range(8)]
        inside = (lane8 >= k) & (lane8 < k + 8)
        unit = jnp.where(lane8 == row8 + k, -1.0, 0.0)
        rows = jnp.where(inside, unit, block[k : k + 8, :])
        pivots = [col[k : k + 8, :] for col in cols]
        for i in range(0, 8, 2):
            a, b, d = pivots[i][i : i + 1], pivots[i][i + 1 : i + 2], pivots[i + 1][i + 1 : i + 2]
            scale = 1.0 / (a * d - b * b)
            a, b, d = d * scale, -b * scale, a * scale

            def solved(x):
                x0, x1 = x[i : i + 1], x[i + 1 : i + 2]
                y0, y1 = a * x0 + b * x1, b * x0 + d * x1
                y = x - pivots[i] * y0 - pivots[i + 1] * y1
                return jnp.where(row8 == i, y0, jnp.where(row8 == i + 1, y1, y))

            rows = solved(rows)
            pivots = [solved(x) if j > i + 1 else x for j, x in enumerate(pivots)]
        parts = [col * rows[i : i + 1] for i, col in enumerate(cols)]
        change = ((parts[0] + parts[1]) + (parts[2] + parts[3])) + (
            (parts[4] + parts[5]) + (parts[6] + parts[7])
        )
        block = jnp.where((lane >= k) & (lane < k + 8), 0.0, block) - change
        pieces = [block[:k]] * (k > 0) + [rows] + [block[k + 8 :]] * (k + 8 < size)
        block = jnp.concatenate(pieces, axis=0)
    return -block


def weights_of(sums_ref, entries):
    summed = jnp.sum(sums_ref[...], axis=0)
    table = {}
    for place, (i, j) in enumerate(PAIRS):
        table[i, j] = table[j, i] = summed[:, place : place + 1]

    def inner(a, b):
        out = 0.0
        for i, x in enumerate(a):
            for j, y in enumerate(b):
                out = out + x * y * table[i, j]
        return out

    def scale_of(squares):
        return lax.rsqrt(squares / entries + epsilon)

    weights = [scale_of(table[0, 0])]
    for _ in range(ITERS):
        up = [0.0 * weights[0]] + [x * (1.0 / SHRINK) for x in weights]
        padded = weights + [0.0 * weights[0]]
        image = [(x - y) * (1.0 / step_size) for x, y in zip(padded, up)]
        rayleigh = inner(weights, image) / (inner(weights, weights) + epsilon)
        update = [y + step_size * rayleigh * x for x, y in zip(padded, up)]
        scale = scale_of(jnp.maximum(inner(update, update), 0.0))
        weights = [x * scale for x in update]
    return weights


def truncate_body(block_rows_ref, ranks_ref, sums_ref, guess_ref, *refs):
    powers = refs[: ITERS - 1]
    last = refs[ITERS - 1 : ITERS + 4]
    slabs = refs[ITERS + 4 : 2 * ITERS + 5]
    slab_ref, cut_ref, state, gram = refs[2 * ITERS + 5 :]
    sector = own_sector()
    slab_rows, width = slab_ref.shape
    capacity = guess_ref.shape[0]
    members = capacity // slab_rows
    weights = weights_of(sums_ref, float(MEAN * block_rows_ref.shape[0] * width))
    live = row_index(guess_ref.shape) < block_rows_ref[sector]
    current = jnp.where(live, guess_ref[...], 0.0) * weights[0]
    for weight, ref in zip(weights[1:], powers):
        current = current + weight * ref[...].astype(jnp.float32)
    state[...] = current
    member = lax.axis_index("mpo")
    own, before, after, far_before, far_after = last
    pieces = [(own, 0), (before, -1), (after, 1)]
    pieces += [(far_before.at[i], -4 + i) for i in range(3)]
    pieces += [(far_after.at[i], 2 + i) for i in range(2)]
    for piece, by in pieces:
        place = lax.rem(member + by + members, members)
        span = pl.ds(pl.multiple_of(place * slab_rows, 8), slab_rows)
        state[span, :] += weights[-1] * piece[...].astype(jnp.float32)
    current = state[...]
    density = dot32(current, current, ((0,), (0,)))
    row = lax.broadcasted_iota(jnp.int32, density.shape, 0)
    lane = lax.broadcasted_iota(jnp.int32, density.shape, 1)
    diagonal = (row == lane).astype(jnp.float32)
    kept = lane < ranks_ref[sector]
    basis = jnp.where(kept, diagonal + density * (1.0 / MEAN), 0.0)
    gram[...] = dot32(basis, basis, ((0,), (0,))) + jnp.where(kept, 0.0, diagonal)
    panel_row = lax.broadcasted_iota(jnp.int32, (BASE, width), 0)
    panel_lane = lax.broadcasted_iota(jnp.int32, (BASE, width), 1)
    for low in range(0, width, BASE):
        panel = gram[low : low + BASE, :]
        inverse = inverse_of(panel[:, low : low + BASE])
        inside = (panel_lane >= low) & (panel_lane < low + BASE)
        select = (panel_lane == panel_row + low).astype(jnp.float32)
        rest = jnp.where(inside, 0.0, panel)
        solved = dot32(inverse, rest, ((1,), (0,)))
        change = dot32(
            jnp.concatenate([rest, solved], axis=0),
            jnp.concatenate([solved, -select], axis=0),
            ((0,), (0,)),
        )
        taken = (lane >= low) & (lane < low + BASE)
        gram[...] = jnp.where(taken, 0.0, gram[...]) - change
        gram[low : low + BASE, :] = solved - dot32(inverse, select, ((1,), (0,)))
    slab = weights[0] * slabs[0][...]
    for weight, ref in zip(weights[1:], slabs[1:]):
        slab = slab + weight * ref[...]
    slab_ref[...] = slab
    coords = dot32(slab, basis, ((1,), (0,)))
    solved = -dot32(coords, gram[...], ((1,), (0,)))
    cut_ref[...] = dot32(solved, basis, ((1,), (1,)))


def passed_along(array, by):
    peers = lax.axis_size("sec")
    return lax.ppermute(array, "sec", [(i, (i + by) % peers) for i in range(peers)])


def swapped(array, senders=(0, 1)):
    peers = lax.axis_size("sec")
    return lax.ppermute(array, "sec", [(i, i ^ 1) for i in range(peers) if i % 2 in senders])


def neighbours(whole, done):
    ahead, behind = passed_along(whole, -2), passed_along(whole, 2)
    whole, done, behind = lax.optimization_barrier((whole, done, behind))
    partner = swapped(whole)
    before = swapped(behind, (1,))
    after = swapped(ahead, (0,))
    return done, partner, before, after, ahead, behind


def shards(guess, left_env, right_env, block_rows, charges, ranks):
    capacity, width = guess.shape
    sectors = block_rows.shape[0]
    members = lax.axis_size("mpo")
    rows = capacity // members
    exact = like((rows, width), jnp.float32)
    sent = like((members, rows, width), jnp.bfloat16)

    def exchanged(array, axis):
        return lax.all_to_all(array, axis, 0, 0, tiled=True)

    def along(array, by):
        return lax.ppermute(array, "mpo", [(i, (i + by) % members) for i in range(members)])

    whole = begin(block_rows, guess)
    powers, slabs = [], []
    for repeat in range(ITERS - 1):
        part = apply_terms(block_rows, charges, whole, left_env, right_env)
        pieces = exchanged(part.reshape(members, rows, width), "mpo")
        if repeat == 0:
            start, new, outgoing = call(
                first_slab_body, "first_slab", (exact, exact, sent), [SMEM, VMEM, VMEM]
            )(block_rows, guess, pieces)
            slabs.append(start)
        else:
            new, outgoing = call(slab_body, "slab", (exact, sent), [VMEM] * 2)(slabs[-1], pieces)
        slabs.append(new)
        whole = exchanged(outgoing, "mpo").reshape(capacity, width)
        powers.append(whole)
    part = apply_terms(block_rows, charges, whole, left_env, right_env)
    pieces = exchanged(part.reshape(members, rows, width), "mpo")
    new, own, tables = call(
        last_slab_body,
        "last_slab",
        (exact, like((rows, width), jnp.bfloat16), like((sectors, 1, 128), jnp.float32)),
        [VMEM] * (ITERS + 1),
    )(*slabs, pieces)
    slabs.append(new)
    before, after = along(own, 1), along(own, -1)
    before, after, sums = lax.optimization_barrier((before, after, exchanged(tables, "sec")))
    far_before = along(jnp.stack([before, own, after]), 3)
    far_after = along(jnp.stack([before, own]), -3)
    sums = call(fold_body, "fold", like((members, 1, 128), jnp.float32), [VMEM])(sums)
    sums = exchanged(sums, "mpo")
    return call(
        truncate_body,
        "truncate",
        (exact, exact),
        [SMEM, SMEM] + [VMEM] * (2 * ITERS + 7),
        [pltpu.VMEM((capacity, width), jnp.float32), pltpu.VMEM((width, width), jnp.float32)],
        limit=24,
    )(block_rows, ranks, sums, guess, *powers, own, before, after, far_before, far_after, *slabs)


def solution(mesh):
    return jax.shard_map(
        shards,
        mesh=mesh,
        in_specs=(P("sec", None), P("mpo", "sec", None), P("mpo", "sec", None), P(), P("mpo"), P()),
        out_specs=(P(("sec", "mpo"), None), P(("sec", "mpo"), None)),
        check_vma=False,
    )
```

```python
import jax
import jax.numpy as jnp
from jax import lax
from jax.experimental import pallas as pl
from jax.experimental.pallas import tpu as pltpu
from jax.sharding import PartitionSpec as P

MEAN = 256
ITERS = 4
REACH = 2
SHRINK = 2.0**-4
epsilon = 1e-06
step_size = 0.1
highest = lax.Precision.HIGHEST
TILE = 256
BASE = 64
PAIRS = [(i, j) for i in range(ITERS + 1) for j in range(i, ITERS + 1)]
SMEM = pl.BlockSpec(memory_space=pltpu.SMEM)
VMEM = pl.BlockSpec(memory_space=pltpu.VMEM)


def call(body, name, out_shape, in_specs, scratch=(), limit=16):
    return pl.pallas_call(
        body,
        in_specs=in_specs,
        out_specs=jax.tree.map(lambda _: VMEM, out_shape),
        out_shape=out_shape,
        scratch_shapes=list(scratch),
        compiler_params=pltpu.CompilerParams(vmem_limit_bytes=limit << 20),
        name=name,
    )


def like(shape, dtype):
    return jax.ShapeDtypeStruct(shape, dtype)


def own_sector():
    return lax.axis_index("sec")


def row_index(shape, base=0):
    return base + lax.broadcasted_iota(jnp.int32, shape, len(shape) - 2)


def begin_body(block_rows_ref, guess_ref, out_ref):
    live = row_index(guess_ref.shape) < block_rows_ref[own_sector()]
    out_ref[...] = jnp.where(live, guess_ref[...], 0.0).astype(out_ref.dtype)


def begin(block_rows, guess):
    return call(begin_body, "begin", like(guess.shape, jnp.bfloat16), [SMEM, VMEM])(
        block_rows, guess
    )


def tile_cases(rows, tiles):
    cases = []
    for i in range(1, tiles + 1):
        fits = rows > (i - 1) * TILE
        cases.append((i * TILE, fits if i == tiles else fits & (rows <= i * TILE)))
    return cases


def middle_of(left, block):
    return jnp.dot(left, block, preferred_element_type=jnp.float32).astype(jnp.bfloat16)


def own_term_body(block_rows_ref, charges_ref, own_ref, left_ref, right_ref, out_ref):
    terms, capacity, _ = left_ref.shape

    def apply_term(term, _):
        for high, fits in tile_cases(block_rows_ref[own_sector()], capacity // TILE):

            @pl.when(fits & (charges_ref[term] == 0))
            def _():
                out_ref[:high, :] = middle_of(left_ref[term, :high, :high], own_ref[:high, :])
        return 0

    lax.fori_loop(0, terms, apply_term, 0)


def terms_body(
    block_rows_ref, charges_ref, done_ref, partner_ref, other_ref, ahead_ref, behind_ref,
    left_ref, right_ref, out_ref, held, middles,
):
    sector = own_sector()
    sectors = block_rows_ref.shape[0]
    core = lax.rem(sector, 2)
    held[0] = ahead_ref[...]
    held[4] = behind_ref[...]
    held[1 + 2 * core] = partner_ref[...]
    held[3 - 2 * core] = other_ref[...]
    terms, capacity, _ = left_ref.shape
    tiles = capacity // TILE
    own_cases = tile_cases(block_rows_ref[sector], tiles)

    def apply_term(term, _):
        charge = charges_ref[term]
        source_rows = block_rows_ref[lax.rem(sector - charge + sectors, sectors)]

        @pl.when(charge == 0)
        def _():
            middles[term] = done_ref[...]

        for high, own_fits in own_cases:
            for wide, source_fits in tile_cases(source_rows, tiles):

                @pl.when(own_fits & source_fits & (charge != 0))
                def _():
                    middles[term, :high, :] = middle_of(
                        left_ref[term, :high, :wide], held[REACH + charge, :wide, :]
                    )
        return 0

    lax.fori_loop(0, terms, apply_term, 0)
    for high, fits in own_cases:

        @pl.when(fits)
        def _():
            total = 0.0
            for term in range(terms):
                total = total + jnp.dot(
                    middles[term, :high, :], right_ref[term], preferred_element_type=jnp.float32
                )
            live = row_index(total.shape) < block_rows_ref[sector]
            out_ref[:high, :] = jnp.where(live, total, 0.0).astype(out_ref.dtype)
            if high < capacity:
                out_ref[high:, :] = jnp.zeros((capacity - high, total.shape[1]), out_ref.dtype)


def apply_terms(block_rows, charges, whole, left_env, right_env):
    terms, capacity, _ = left_env.shape
    width = right_env.shape[-1]
    block = like((capacity, width), jnp.bfloat16)
    done = call(own_term_body, "own_term", block, [SMEM, SMEM] + [VMEM] * 3)(
        block_rows, charges, whole, left_env, right_env
    )
    return call(
        terms_body,
        "apply_terms",
        block,
        [SMEM, SMEM] + [VMEM] * 7,
        [
            pltpu.VMEM((2 * REACH + 1, capacity, width), jnp.bfloat16),
            pltpu.VMEM((terms, capacity, width), jnp.bfloat16),
        ],
    )(block_rows, charges, *neighbours(whole, done), left_env, right_env)


def next_slab(pieces_ref, slab):
    applied = jnp.sum(pieces_ref[...].astype(jnp.float32), axis=0)
    return (slab - step_size * applied) * SHRINK


def first_slab_body(block_rows_ref, guess_ref, pieces_ref, start_ref, new_ref, sent_ref):
    rows = start_ref.shape[0]
    base = pl.multiple_of(lax.axis_index("mpo") * rows, 8)
    slab = guess_ref[pl.ds(base, rows), :]
    slab = jnp.where(row_index(slab.shape, base) < block_rows_ref[own_sector()], slab, 0.0)
    start_ref[...] = slab
    new = next_slab(pieces_ref, slab)
    new_ref[...] = new
    sent_ref[...] = jnp.broadcast_to(new.astype(sent_ref.dtype)[None], sent_ref.shape)


def slab_body(slab_ref, pieces_ref, new_ref, sent_ref):
    new = next_slab(pieces_ref, slab_ref[...])
    new_ref[...] = new
    sent_ref[...] = jnp.broadcast_to(new.astype(sent_ref.dtype)[None], sent_ref.shape)


def last_slab_body(*refs):
    slab_refs, (pieces_ref, new_ref, sent_ref, table_ref) = refs[:ITERS], refs[ITERS:]
    slabs = [ref[...] for ref in slab_refs]
    new = next_slab(pieces_ref, slabs[-1])
    new_ref[...] = new
    sent_ref[...] = new.astype(sent_ref.dtype)
    slabs.append(new)
    lane = lax.broadcasted_iota(jnp.int32, (1, 128), 1)
    table = jnp.zeros((1, 128), jnp.float32)
    for place, (i, j) in enumerate(PAIRS):
        value = jnp.sum(jnp.sum(slabs[i] * slabs[j], axis=0, keepdims=True), axis=1, keepdims=True)
        table = table + jnp.where(lane == place, value, 0.0)
    table_ref[...] = jnp.broadcast_to(table[None], table_ref.shape)


def fold_body(tables_ref, out_ref):
    out_ref[...] = jnp.broadcast_to(
        jnp.sum(tables_ref[...], axis=0, keepdims=True), out_ref.shape
    )


def dot32(a, b, dims):
    return lax.dot_general(
        a, b, (dims, ((), ())), precision=highest, preferred_element_type=jnp.float32
    )


def inverse_of(block):
    size = block.shape[0]
    lane = lax.broadcasted_iota(jnp.int32, block.shape, 1)
    row8 = lax.broadcasted_iota(jnp.int32, (8, size), 0)
    lane8 = lane[:8]
    for k in range(0, size, 8):
        cols = [jnp.broadcast_to(block[:, k + i : k + i + 1], block.shape) for i in range(8)]
        inside = (lane8 >= k) & (lane8 < k + 8)
        unit = jnp.where(lane8 == row8 + k, -1.0, 0.0)
        rows = jnp.where(inside, unit, block[k : k + 8, :])
        pivots = [col[k : k + 8, :] for col in cols]
        for i in range(0, 8, 2):
            a, b, d = pivots[i][i : i + 1], pivots[i][i + 1 : i + 2], pivots[i + 1][i + 1 : i + 2]
            scale = 1.0 / (a * d - b * b)
            a, b, d = d * scale, -b * scale, a * scale

            def solved(x):
                x0, x1 = x[i : i + 1], x[i + 1 : i + 2]
                y0, y1 = a * x0 + b * x1, b * x0 + d * x1
                y = x - pivots[i] * y0 - pivots[i + 1] * y1
                return jnp.where(row8 == i, y0, jnp.where(row8 == i + 1, y1, y))

            rows = solved(rows)
            pivots = [solved(x) if j > i + 1 else x for j, x in enumerate(pivots)]
        parts = [col * rows[i : i + 1] for i, col in enumerate(cols)]
        change = ((parts[0] + parts[1]) + (parts[2] + parts[3])) + (
            (parts[4] + parts[5]) + (parts[6] + parts[7])
        )
        block = jnp.where((lane >= k) & (lane < k + 8), 0.0, block) - change
        pieces = [block[:k]] * (k > 0) + [rows] + [block[k + 8 :]] * (k + 8 < size)
        block = jnp.concatenate(pieces, axis=0)
    return -block


def weights_of(sums_ref, entries):
    summed = jnp.sum(sums_ref[...], axis=0)
    table = {}
    for place, (i, j) in enumerate(PAIRS):
        table[i, j] = table[j, i] = summed[:, place : place + 1]

    def inner(a, b):
        out = 0.0
        for i, x in enumerate(a):
            for j, y in enumerate(b):
                out = out + x * y * table[i, j]
        return out

    def scale_of(squares):
        return lax.rsqrt(squares / entries + epsilon)

    weights = [scale_of(table[0, 0])]
    for _ in range(ITERS):
        up = [0.0 * weights[0]] + [x * (1.0 / SHRINK) for x in weights]
        padded = weights + [0.0 * weights[0]]
        image = [(x - y) * (1.0 / step_size) for x, y in zip(padded, up)]
        rayleigh = inner(weights, image) / (inner(weights, weights) + epsilon)
        update = [y + step_size * rayleigh * x for x, y in zip(padded, up)]
        scale = scale_of(jnp.maximum(inner(update, update), 0.0))
        weights = [x * scale for x in update]
    return weights


def truncate_body(block_rows_ref, ranks_ref, sums_ref, guess_ref, *refs):
    powers = refs[: ITERS - 1]
    last = refs[ITERS - 1 : ITERS + 4]
    slabs = refs[ITERS + 4 : 2 * ITERS + 5]
    slab_ref, cut_ref, state, gram = refs[2 * ITERS + 5 :]
    sector = own_sector()
    slab_rows, width = slab_ref.shape
    capacity = guess_ref.shape[0]
    members = capacity // slab_rows
    weights = weights_of(sums_ref, float(MEAN * block_rows_ref.shape[0] * width))
    live = row_index(guess_ref.shape) < block_rows_ref[sector]
    current = jnp.where(live, guess_ref[...], 0.0) * weights[0]
    for weight, ref in zip(weights[1:], powers):
        current = current + weight * ref[...].astype(jnp.float32)
    state[...] = current
    member = lax.axis_index("mpo")
    own, before, after, far_before, far_after = last
    pieces = [(own, 0), (before, -1), (after, 1)]
    pieces += [(far_before.at[i], -4 + i) for i in range(3)]
    pieces += [(far_after.at[i], 2 + i) for i in range(2)]
    for piece, by in pieces:
        place = lax.rem(member + by + members, members)
        span = pl.ds(pl.multiple_of(place * slab_rows, 8), slab_rows)
        state[span, :] += weights[-1] * piece[...].astype(jnp.float32)
    current = state[...]
    density = dot32(current, current, ((0,), (0,)))
    row = lax.broadcasted_iota(jnp.int32, density.shape, 0)
    lane = lax.broadcasted_iota(jnp.int32, density.shape, 1)
    diagonal = (row == lane).astype(jnp.float32)
    kept = lane < ranks_ref[sector]
    basis = jnp.where(kept, diagonal + density * (1.0 / MEAN), 0.0)
    gram[...] = dot32(basis, basis, ((0,), (0,))) + jnp.where(kept, 0.0, diagonal)
    panel_row = lax.broadcasted_iota(jnp.int32, (BASE, width), 0)
    panel_lane = lax.broadcasted_iota(jnp.int32, (BASE, width), 1)
    for low in range(0, width, BASE):
        panel = gram[low : low + BASE, :]
        inverse = inverse_of(panel[:, low : low + BASE])
        inside = (panel_lane >= low) & (panel_lane < low + BASE)
        select = (panel_lane == panel_row + low).astype(jnp.float32)
        rest = jnp.where(inside, 0.0, panel)
        solved = dot32(inverse, rest, ((1,), (0,)))
        change = dot32(
            jnp.concatenate([rest, solved], axis=0),
            jnp.concatenate([solved, -select], axis=0),
            ((0,), (0,)),
        )
        taken = (lane >= low) & (lane < low + BASE)
        gram[...] = jnp.where(taken, 0.0, gram[...]) - change
        gram[low : low + BASE, :] = solved - dot32(inverse, select, ((1,), (0,)))
    slab = weights[0] * slabs[0][...]
    for weight, ref in zip(weights[1:], slabs[1:]):
        slab = slab + weight * ref[...]
    slab_ref[...] = slab
    coords = dot32(slab, basis, ((1,), (0,)))
    solved = -dot32(coords, gram[...], ((1,), (0,)))
    cut_ref[...] = dot32(solved, basis, ((1,), (1,)))


def passed_along(array, by):
    peers = lax.axis_size("sec")
    return lax.ppermute(array, "sec", [(i, (i + by) % peers) for i in range(peers)])


def swapped(array):
    peers = lax.axis_size("sec")
    return lax.ppermute(array, "sec", [(i, i ^ 1) for i in range(peers)])


def neighbours(whole, done):
    ahead, behind = passed_along(whole, -2), passed_along(whole, 2)
    whole, done, ahead, behind = lax.optimization_barrier((whole, done, ahead, behind))
    partner = swapped(whole)
    other = swapped(jnp.where(own_sector() % 2 == 0, ahead, behind))
    return done, partner, other, ahead, behind


def shards(guess, left_env, right_env, block_rows, charges, ranks):
    capacity, width = guess.shape
    sectors = block_rows.shape[0]
    members = lax.axis_size("mpo")
    rows = capacity // members
    exact = like((rows, width), jnp.float32)
    sent = like((members, rows, width), jnp.bfloat16)

    def exchanged(array, axis):
        return lax.all_to_all(array, axis, 0, 0, tiled=True)

    def along(array, by):
        return lax.ppermute(array, "mpo", [(i, (i + by) % members) for i in range(members)])

    whole = begin(block_rows, guess)
    powers, slabs = [], []
    for repeat in range(ITERS - 1):
        part = apply_terms(block_rows, charges, whole, left_env, right_env)
        pieces = exchanged(part.reshape(members, rows, width), "mpo")
        if repeat == 0:
            start, new, outgoing = call(
                first_slab_body, "first_slab", (exact, exact, sent), [SMEM, VMEM, VMEM]
            )(block_rows, guess, pieces)
            slabs.append(start)
        else:
            new, outgoing = call(slab_body, "slab", (exact, sent), [VMEM] * 2)(slabs[-1], pieces)
        slabs.append(new)
        whole = exchanged(outgoing, "mpo").reshape(capacity, width)
        powers.append(whole)
    part = apply_terms(block_rows, charges, whole, left_env, right_env)
    pieces = exchanged(part.reshape(members, rows, width), "mpo")
    new, own, tables = call(
        last_slab_body,
        "last_slab",
        (exact, like((rows, width), jnp.bfloat16), like((sectors, 1, 128), jnp.float32)),
        [VMEM] * (ITERS + 1),
    )(*slabs, pieces)
    slabs.append(new)
    before, after = along(own, 1), along(own, -1)
    before, after, sums = lax.optimization_barrier((before, after, exchanged(tables, "sec")))
    far_before = along(jnp.stack([before, own, after]), 3)
    far_after = along(jnp.stack([before, own]), -3)
    sums = call(fold_body, "fold", like((members, 1, 128), jnp.float32), [VMEM])(sums)
    sums = exchanged(sums, "mpo")
    return call(
        truncate_body,
        "truncate",
        (exact, exact),
        [SMEM, SMEM] + [VMEM] * (2 * ITERS + 7),
        [pltpu.VMEM((capacity, width), jnp.float32), pltpu.VMEM((width, width), jnp.float32)],
        limit=24,
    )(block_rows, ranks, sums, guess, *powers, own, before, after, far_before, far_after, *slabs)


def solution(mesh):
    return jax.shard_map(
        shards,
        mesh=mesh,
        in_specs=(P("sec", None), P("mpo", "sec", None), P("mpo", "sec", None), P(), P("mpo"), P()),
        out_specs=(P(("sec", "mpo"), None), P(("sec", "mpo"), None)),
        check_vma=False,
    )
```

```python
import jax
import jax.numpy as jnp
from jax import lax
from jax.experimental import pallas as pl
from jax.experimental.pallas import tpu as pltpu
from jax.sharding import PartitionSpec as P

MEAN = 256
ITERS = 4
REACH = 2
SHRINK = 2.0**-4
epsilon = 1e-06
step_size = 0.1
highest = lax.Precision.HIGHEST
TILE = 256
BASE = 64
PAIRS = [(i, j) for i in range(ITERS + 1) for j in range(i, ITERS + 1)]
SMEM = pl.BlockSpec(memory_space=pltpu.SMEM)
VMEM = pl.BlockSpec(memory_space=pltpu.VMEM)


def call(body, name, out_shape, in_specs, scratch=(), limit=16):
    return pl.pallas_call(
        body,
        in_specs=in_specs,
        out_specs=jax.tree.map(lambda _: VMEM, out_shape),
        out_shape=out_shape,
        scratch_shapes=list(scratch),
        compiler_params=pltpu.CompilerParams(vmem_limit_bytes=limit << 20),
        name=name,
    )


def like(shape, dtype):
    return jax.ShapeDtypeStruct(shape, dtype)


def own_sector():
    return lax.axis_index("sec")


def row_index(shape, base=0):
    return base + lax.broadcasted_iota(jnp.int32, shape, len(shape) - 2)


def begin_body(block_rows_ref, guess_ref, out_ref):
    live = row_index(guess_ref.shape) < block_rows_ref[own_sector()]
    out_ref[...] = jnp.where(live, guess_ref[...], 0.0).astype(out_ref.dtype)


def begin(block_rows, guess):
    return call(begin_body, "begin", like(guess.shape, jnp.bfloat16), [SMEM, VMEM])(
        block_rows, guess
    )


def tile_cases(rows, tiles):
    cases = []
    for i in range(1, tiles + 1):
        fits = rows > (i - 1) * TILE
        cases.append((i * TILE, fits if i == tiles else fits & (rows <= i * TILE)))
    return cases


def middle_of(left, block):
    return jnp.dot(left, block, preferred_element_type=jnp.float32).astype(jnp.bfloat16)


def term_of(charges_ref, charge):
    place = 0
    for term in range(1, charges_ref.shape[0]):
        place = jnp.where(charges_ref[term] == charge, term, place)
    return place


def middle_into(target, block_rows_ref, charges_ref, charge, block_ref, left_ref):
    sector = own_sector()
    sectors = block_rows_ref.shape[0]
    source_rows = block_rows_ref[lax.rem(sector - charge + sectors, sectors)]
    term = term_of(charges_ref, charge)
    tiles = left_ref.shape[1] // TILE
    for high, own_fits in tile_cases(block_rows_ref[sector], tiles):
        for wide, source_fits in tile_cases(source_rows, tiles):

            @pl.when(own_fits & source_fits)
            def _():
                target[:high, :] = middle_of(left_ref[term, :high, :wide], block_ref[:wide, :])


def own_term_body(block_rows_ref, charges_ref, own_ref, left_ref, out_ref):
    term = term_of(charges_ref, 0)
    tiles = left_ref.shape[1] // TILE
    for high, fits in tile_cases(block_rows_ref[own_sector()], tiles):

        @pl.when(fits)
        def _():
            out_ref[:high, :] = middle_of(left_ref[term, :high, :high], own_ref[:high, :])


def summed(pairs, right_ref, high):
    total = 0.0
    for middle, term in pairs:
        total = total + jnp.dot(
            middle[:high, :], right_ref[term], preferred_element_type=jnp.float32
        )
    return total


def far_terms_body(
    block_rows_ref, charges_ref, done_ref, ahead_ref, behind_ref, left_ref, right_ref, out_ref,
    ahead_middle, behind_middle,
):
    middle_into(ahead_middle, block_rows_ref, charges_ref, -REACH, ahead_ref, left_ref)
    middle_into(behind_middle, block_rows_ref, charges_ref, REACH, behind_ref, left_ref)
    pairs = [(done_ref, 0), (ahead_middle, -REACH), (behind_middle, REACH)]
    pairs = [(middle, term_of(charges_ref, charge)) for middle, charge in pairs]
    for high, fits in tile_cases(block_rows_ref[own_sector()], left_ref.shape[1] // TILE):

        @pl.when(fits)
        def _():
            out_ref[:high, :] = summed(pairs, right_ref, high)


def near_terms_body(
    block_rows_ref, charges_ref, sum_ref, partner_ref, other_ref, left_ref, right_ref, out_ref,
    partner_middle, other_middle,
):
    sector = own_sector()
    near = jnp.where(lax.rem(sector, 2) == 0, -1, 1)
    middle_into(partner_middle, block_rows_ref, charges_ref, near, partner_ref, left_ref)
    middle_into(other_middle, block_rows_ref, charges_ref, -near, other_ref, left_ref)
    pairs = [
        (partner_middle, term_of(charges_ref, near)),
        (other_middle, term_of(charges_ref, -near)),
    ]
    capacity, width = out_ref.shape
    own_rows = block_rows_ref[sector]
    for high, fits in tile_cases(own_rows, capacity // TILE):

        @pl.when(fits)
        def _():
            total = sum_ref[:high, :] + summed(pairs, right_ref, high)
            live = row_index(total.shape) < own_rows
            out_ref[:high, :] = jnp.where(live, total, 0.0).astype(out_ref.dtype)
            if high < capacity:
                out_ref[high:, :] = jnp.zeros((capacity - high, width), out_ref.dtype)


def apply_terms(block_rows, charges, whole, left_env, right_env):
    terms, capacity, _ = left_env.shape
    width = right_env.shape[-1]
    block = like((capacity, width), jnp.bfloat16)
    middles = [pltpu.VMEM((capacity, width), jnp.bfloat16)] * 2
    ahead, behind = passed_along(whole, -2), passed_along(whole, 2)
    done = call(own_term_body, "own_term", block, [SMEM, SMEM] + [VMEM] * 2)(
        block_rows, charges, whole, left_env
    )
    whole, done, ahead, behind = lax.optimization_barrier((whole, done, ahead, behind))
    partner = swapped(whole)
    other = swapped(jnp.where(own_sector() % 2 == 0, ahead, behind))
    partial = call(
        far_terms_body,
        "far_terms",
        like((capacity, width), jnp.float32),
        [SMEM, SMEM] + [VMEM] * 5,
        middles,
    )(block_rows, charges, done, ahead, behind, left_env, right_env)
    return call(near_terms_body, "near_terms", block, [SMEM, SMEM] + [VMEM] * 5, middles)(
        block_rows, charges, partial, partner, other, left_env, right_env
    )


def next_slab(pieces_ref, slab):
    applied = jnp.sum(pieces_ref[...].astype(jnp.float32), axis=0)
    return (slab - step_size * applied) * SHRINK


def first_slab_body(block_rows_ref, guess_ref, pieces_ref, start_ref, new_ref, sent_ref):
    rows = start_ref.shape[0]
    base = pl.multiple_of(lax.axis_index("mpo") * rows, 8)
    slab = guess_ref[pl.ds(base, rows), :]
    slab = jnp.where(row_index(slab.shape, base) < block_rows_ref[own_sector()], slab, 0.0)
    start_ref[...] = slab
    new = next_slab(pieces_ref, slab)
    new_ref[...] = new
    sent_ref[...] = jnp.broadcast_to(new.astype(sent_ref.dtype)[None], sent_ref.shape)


def slab_body(slab_ref, pieces_ref, new_ref, sent_ref):
    new = next_slab(pieces_ref, slab_ref[...])
    new_ref[...] = new
    sent_ref[...] = jnp.broadcast_to(new.astype(sent_ref.dtype)[None], sent_ref.shape)


def last_slab_body(*refs):
    slab_refs, (pieces_ref, new_ref, sent_ref, table_ref) = refs[:ITERS], refs[ITERS:]
    slabs = [ref[...] for ref in slab_refs]
    new = next_slab(pieces_ref, slabs[-1])
    new_ref[...] = new
    sent_ref[...] = new.astype(sent_ref.dtype)
    slabs.append(new)
    lane = lax.broadcasted_iota(jnp.int32, (1, 128), 1)
    table = jnp.zeros((1, 128), jnp.float32)
    for place, (i, j) in enumerate(PAIRS):
        value = jnp.sum(jnp.sum(slabs[i] * slabs[j], axis=0, keepdims=True), axis=1, keepdims=True)
        table = table + jnp.where(lane == place, value, 0.0)
    table_ref[...] = jnp.broadcast_to(table[None], table_ref.shape)


def fold_body(tables_ref, out_ref):
    out_ref[...] = jnp.broadcast_to(
        jnp.sum(tables_ref[...], axis=0, keepdims=True), out_ref.shape
    )


def dot32(a, b, dims):
    return lax.dot_general(
        a, b, (dims, ((), ())), precision=highest, preferred_element_type=jnp.float32
    )


def inverse_of(block):
    size = block.shape[0]
    lane = lax.broadcasted_iota(jnp.int32, block.shape, 1)
    row8 = lax.broadcasted_iota(jnp.int32, (8, size), 0)
    lane8 = lane[:8]
    for k in range(0, size, 8):
        cols = [jnp.broadcast_to(block[:, k + i : k + i + 1], block.shape) for i in range(8)]
        inside = (lane8 >= k) & (lane8 < k + 8)
        unit = jnp.where(lane8 == row8 + k, -1.0, 0.0)
        rows = jnp.where(inside, unit, block[k : k + 8, :])
        pivots = [col[k : k + 8, :] for col in cols]
        for i in range(0, 8, 2):
            a, b, d = pivots[i][i : i + 1], pivots[i][i + 1 : i + 2], pivots[i + 1][i + 1 : i + 2]
            scale = 1.0 / (a * d - b * b)
            a, b, d = d * scale, -b * scale, a * scale

            def solved(x):
                x0, x1 = x[i : i + 1], x[i + 1 : i + 2]
                y0, y1 = a * x0 + b * x1, b * x0 + d * x1
                y = x - pivots[i] * y0 - pivots[i + 1] * y1
                return jnp.where(row8 == i, y0, jnp.where(row8 == i + 1, y1, y))

            rows = solved(rows)
            pivots = [solved(x) if j > i + 1 else x for j, x in enumerate(pivots)]
        parts = [col * rows[i : i + 1] for i, col in enumerate(cols)]
        change = ((parts[0] + parts[1]) + (parts[2] + parts[3])) + (
            (parts[4] + parts[5]) + (parts[6] + parts[7])
        )
        block = jnp.where((lane >= k) & (lane < k + 8), 0.0, block) - change
        pieces = [block[:k]] * (k > 0) + [rows] + [block[k + 8 :]] * (k + 8 < size)
        block = jnp.concatenate(pieces, axis=0)
    return -block


def weights_of(sums_ref, entries):
    summed = jnp.sum(sums_ref[...], axis=0)
    table = {}
    for place, (i, j) in enumerate(PAIRS):
        table[i, j] = table[j, i] = summed[:, place : place + 1]

    def inner(a, b):
        out = 0.0
        for i, x in enumerate(a):
            for j, y in enumerate(b):
                out = out + x * y * table[i, j]
        return out

    def scale_of(squares):
        return lax.rsqrt(squares / entries + epsilon)

    weights = [scale_of(table[0, 0])]
    for _ in range(ITERS):
        up = [0.0 * weights[0]] + [x * (1.0 / SHRINK) for x in weights]
        padded = weights + [0.0 * weights[0]]
        image = [(x - y) * (1.0 / step_size) for x, y in zip(padded, up)]
        rayleigh = inner(weights, image) / (inner(weights, weights) + epsilon)
        update = [y + step_size * rayleigh * x for x, y in zip(padded, up)]
        scale = scale_of(jnp.maximum(inner(update, update), 0.0))
        weights = [x * scale for x in update]
    return weights


def truncate_body(block_rows_ref, ranks_ref, sums_ref, guess_ref, *refs):
    powers = refs[: ITERS - 1]
    last = refs[ITERS - 1 : ITERS + 4]
    slabs = refs[ITERS + 4 : 2 * ITERS + 5]
    slab_ref, cut_ref, state, gram = refs[2 * ITERS + 5 :]
    sector = own_sector()
    slab_rows, width = slab_ref.shape
    capacity = guess_ref.shape[0]
    members = capacity // slab_rows
    weights = weights_of(sums_ref, float(MEAN * block_rows_ref.shape[0] * width))
    live = row_index(guess_ref.shape) < block_rows_ref[sector]
    current = jnp.where(live, guess_ref[...], 0.0) * weights[0]
    for weight, ref in zip(weights[1:], powers):
        current = current + weight * ref[...].astype(jnp.float32)
    state[...] = current
    member = lax.axis_index("mpo")
    own, before, after, far_before, far_after = last
    pieces = [(own, 0), (before, -1), (after, 1)]
    pieces += [(far_before.at[i], -4 + i) for i in range(3)]
    pieces += [(far_after.at[i], 2 + i) for i in range(2)]
    for piece, by in pieces:
        place = lax.rem(member + by + members, members)
        span = pl.ds(pl.multiple_of(place * slab_rows, 8), slab_rows)
        state[span, :] += weights[-1] * piece[...].astype(jnp.float32)
    current = state[...]
    density = dot32(current, current, ((0,), (0,)))
    row = lax.broadcasted_iota(jnp.int32, density.shape, 0)
    lane = lax.broadcasted_iota(jnp.int32, density.shape, 1)
    diagonal = (row == lane).astype(jnp.float32)
    kept = lane < ranks_ref[sector]
    basis = jnp.where(kept, diagonal + density * (1.0 / MEAN), 0.0)
    gram[...] = dot32(basis, basis, ((0,), (0,))) + jnp.where(kept, 0.0, diagonal)
    panel_row = lax.broadcasted_iota(jnp.int32, (BASE, width), 0)
    panel_lane = lax.broadcasted_iota(jnp.int32, (BASE, width), 1)
    for low in range(0, width, BASE):
        panel = gram[low : low + BASE, :]
        inverse = inverse_of(panel[:, low : low + BASE])
        inside = (panel_lane >= low) & (panel_lane < low + BASE)
        select = (panel_lane == panel_row + low).astype(jnp.float32)
        rest = jnp.where(inside, 0.0, panel)
        solved = dot32(inverse, rest, ((1,), (0,)))
        change = dot32(
            jnp.concatenate([rest, solved], axis=0),
            jnp.concatenate([solved, -select], axis=0),
            ((0,), (0,)),
        )
        taken = (lane >= low) & (lane < low + BASE)
        gram[...] = jnp.where(taken, 0.0, gram[...]) - change
        gram[low : low + BASE, :] = solved - dot32(inverse, select, ((1,), (0,)))
    slab = weights[0] * slabs[0][...]
    for weight, ref in zip(weights[1:], slabs[1:]):
        slab = slab + weight * ref[...]
    slab_ref[...] = slab
    coords = dot32(slab, basis, ((1,), (0,)))
    solved = -dot32(coords, gram[...], ((1,), (0,)))
    cut_ref[...] = dot32(solved, basis, ((1,), (1,)))


def passed_along(array, by):
    peers = lax.axis_size("sec")
    return lax.ppermute(array, "sec", [(i, (i + by) % peers) for i in range(peers)])


def swapped(array):
    peers = lax.axis_size("sec")
    return lax.ppermute(array, "sec", [(i, i ^ 1) for i in range(peers)])


def shards(guess, left_env, right_env, block_rows, charges, ranks):
    capacity, width = guess.shape
    sectors = block_rows.shape[0]
    members = lax.axis_size("mpo")
    rows = capacity // members
    exact = like((rows, width), jnp.float32)
    sent = like((members, rows, width), jnp.bfloat16)

    def exchanged(array, axis):
        return lax.all_to_all(array, axis, 0, 0, tiled=True)

    def along(array, by):
        return lax.ppermute(array, "mpo", [(i, (i + by) % members) for i in range(members)])

    whole = begin(block_rows, guess)
    powers, slabs = [], []
    for repeat in range(ITERS - 1):
        part = apply_terms(block_rows, charges, whole, left_env, right_env)
        pieces = exchanged(part.reshape(members, rows, width), "mpo")
        if repeat == 0:
            start, new, outgoing = call(
                first_slab_body, "first_slab", (exact, exact, sent), [SMEM, VMEM, VMEM]
            )(block_rows, guess, pieces)
            slabs.append(start)
        else:
            new, outgoing = call(slab_body, "slab", (exact, sent), [VMEM] * 2)(slabs[-1], pieces)
        slabs.append(new)
        whole = exchanged(outgoing, "mpo").reshape(capacity, width)
        powers.append(whole)
    part = apply_terms(block_rows, charges, whole, left_env, right_env)
    pieces = exchanged(part.reshape(members, rows, width), "mpo")
    new, own, tables = call(
        last_slab_body,
        "last_slab",
        (exact, like((rows, width), jnp.bfloat16), like((sectors, 1, 128), jnp.float32)),
        [VMEM] * (ITERS + 1),
    )(*slabs, pieces)
    slabs.append(new)
    before, after = along(own, 1), along(own, -1)
    before, after, sums = lax.optimization_barrier((before, after, exchanged(tables, "sec")))
    far_before = along(jnp.stack([before, own, after]), 3)
    far_after = along(jnp.stack([before, own]), -3)
    sums = call(fold_body, "fold", like((members, 1, 128), jnp.float32), [VMEM])(sums)
    sums = exchanged(sums, "mpo")
    return call(
        truncate_body,
        "truncate",
        (exact, exact),
        [SMEM, SMEM] + [VMEM] * (2 * ITERS + 7),
        [pltpu.VMEM((capacity, width), jnp.float32), pltpu.VMEM((width, width), jnp.float32)],
        limit=24,
    )(block_rows, ranks, sums, guess, *powers, own, before, after, far_before, far_after, *slabs)


def solution(mesh):
    return jax.shard_map(
        shards,
        mesh=mesh,
        in_specs=(P("sec", None), P("mpo", "sec", None), P("mpo", "sec", None), P(), P("mpo"), P()),
        out_specs=(P(("sec", "mpo"), None), P(("sec", "mpo"), None)),
        check_vma=False,
    )
```

```python
import functools

import jax
import jax.numpy as jnp
from jax import lax
from jax.experimental import pallas as pl
from jax.experimental.pallas import tpu as pltpu
from jax.sharding import PartitionSpec as P

MEAN = 256
ITERS = 4
REACH = 2
SHRINK = 2.0**-4
epsilon = 1e-06
step_size = 0.1
highest = lax.Precision.HIGHEST
TILE = 256
BASE = 64
PANEL = 16
PAIRS = [(i, j) for i in range(ITERS + 1) for j in range(i, ITERS + 1)]
SMEM = pl.BlockSpec(memory_space=pltpu.SMEM)
VMEM = pl.BlockSpec(memory_space=pltpu.VMEM)


def call(body, name, out_shape, in_specs, scratch=(), limit=16):
    return pl.pallas_call(
        body,
        in_specs=in_specs,
        out_specs=jax.tree.map(lambda _: VMEM, out_shape),
        out_shape=out_shape,
        scratch_shapes=list(scratch),
        compiler_params=pltpu.CompilerParams(vmem_limit_bytes=limit << 20),
        name=name,
    )


def like(shape, dtype):
    return jax.ShapeDtypeStruct(shape, dtype)


def own_sector():
    return lax.axis_index("sec")


def row_index(shape, base=0):
    return base + lax.broadcasted_iota(jnp.int32, shape, len(shape) - 2)


def begin_body(block_rows_ref, guess_ref, out_ref):
    live = row_index(guess_ref.shape) < block_rows_ref[own_sector()]
    out_ref[...] = jnp.where(live, guess_ref[...], 0.0).astype(out_ref.dtype)


def begin(block_rows, guess):
    return call(begin_body, "begin", like(guess.shape, jnp.bfloat16), [SMEM, VMEM])(
        block_rows, guess
    )


def tile_cases(rows, tiles):
    cases = []
    for i in range(1, tiles + 1):
        fits = rows > (i - 1) * TILE
        cases.append((i * TILE, fits if i == tiles else fits & (rows <= i * TILE)))
    return cases


def middle_of(left, block):
    return jnp.dot(left, block, preferred_element_type=jnp.float32).astype(jnp.bfloat16)


def term_of(charges_ref, charge):
    place = 0
    for term in range(1, charges_ref.shape[0]):
        place = jnp.where(charges_ref[term] == charge, term, place)
    return place


def middle_into(target, block_rows_ref, charges_ref, charge, block_ref, left_ref):
    sector = own_sector()
    sectors = block_rows_ref.shape[0]
    source_rows = block_rows_ref[lax.rem(sector - charge + sectors, sectors)]
    term = term_of(charges_ref, charge)
    tiles = left_ref.shape[1] // TILE
    for high, own_fits in tile_cases(block_rows_ref[sector], tiles):
        for wide, source_fits in tile_cases(source_rows, tiles):

            @pl.when(own_fits & source_fits)
            def _():
                target[:high, :] = middle_of(left_ref[term, :high, :wide], block_ref[:wide, :])


def summed(pairs, right_ref, high):
    total = 0.0
    for middle, term in pairs:
        total = total + jnp.dot(
            middle[:high, :], right_ref[term], preferred_element_type=jnp.float32
        )
    return total


def near_charge():
    return jnp.where(lax.rem(own_sector(), 2) == 0, -1, 1)


def two_terms_body(charges_of, adds, *refs):
    block_rows_ref, charges_ref, *sums = refs[: 2 + adds]
    *block_refs, left_ref, right_ref, out_ref = refs[2 + adds : -2]
    middles = refs[-2:]
    charges = charges_of()
    for middle, charge, block_ref in zip(middles, charges, block_refs):
        middle_into(middle, block_rows_ref, charges_ref, charge, block_ref, left_ref)
    pairs = [(middle, term_of(charges_ref, charge)) for middle, charge in zip(middles, charges)]
    for high, fits in tile_cases(block_rows_ref[own_sector()], left_ref.shape[1] // TILE):

        @pl.when(fits)
        def _():
            total = summed(pairs, right_ref, high)
            out_ref[:high, :] = sums[0][:high, :] + total if adds else total


def last_term_body(
    block_rows_ref, charges_ref, sum_ref, other_ref, left_ref, right_ref, out_ref, middle
):
    charge = -near_charge()
    middle_into(middle, block_rows_ref, charges_ref, charge, other_ref, left_ref)
    pairs = [(middle, term_of(charges_ref, charge))]
    capacity, width = out_ref.shape
    own_rows = block_rows_ref[own_sector()]
    for high, fits in tile_cases(own_rows, capacity // TILE):

        @pl.when(fits)
        def _():
            total = sum_ref[:high, :] + summed(pairs, right_ref, high)
            live = row_index(total.shape) < own_rows
            out_ref[:high, :] = jnp.where(live, total, 0.0).astype(out_ref.dtype)
            if high < capacity:
                out_ref[high:, :] = jnp.zeros((capacity - high, width), out_ref.dtype)


def apply_terms(block_rows, charges, whole, left_env, right_env):
    terms, capacity, _ = left_env.shape
    width = right_env.shape[-1]
    shape = (capacity, width)
    middle = pltpu.VMEM(shape, jnp.bfloat16)
    ahead, behind = passed_along(whole, -2), passed_along(whole, 2)
    partner = swapped(whole)
    near = call(
        functools.partial(two_terms_body, lambda: (0, near_charge()), 0),
        "near_terms",
        like(shape, jnp.float32),
        [SMEM, SMEM] + [VMEM] * 4,
        [middle] * 2,
    )(block_rows, charges, whole, partner, left_env, right_env)
    near, ahead, behind = lax.optimization_barrier((near, ahead, behind))
    other = swapped(jnp.where(own_sector() % 2 == 0, ahead, behind))
    partial = call(
        functools.partial(two_terms_body, lambda: (-REACH, REACH), 1),
        "far_terms",
        like(shape, jnp.float32),
        [SMEM, SMEM] + [VMEM] * 5,
        [middle] * 2,
    )(block_rows, charges, near, ahead, behind, left_env, right_env)
    return call(
        last_term_body,
        "last_term",
        like(shape, jnp.bfloat16),
        [SMEM, SMEM] + [VMEM] * 4,
        [middle],
    )(block_rows, charges, partial, other, left_env, right_env)


def next_slab(pieces_ref, slab):
    applied = jnp.sum(pieces_ref[...].astype(jnp.float32), axis=0)
    return (slab - step_size * applied) * SHRINK


def first_slab_body(block_rows_ref, guess_ref, pieces_ref, start_ref, new_ref, sent_ref):
    rows = start_ref.shape[0]
    base = pl.multiple_of(lax.axis_index("mpo") * rows, 8)
    slab = guess_ref[pl.ds(base, rows), :]
    slab = jnp.where(row_index(slab.shape, base) < block_rows_ref[own_sector()], slab, 0.0)
    start_ref[...] = slab
    new = next_slab(pieces_ref, slab)
    new_ref[...] = new
    sent_ref[...] = jnp.broadcast_to(new.astype(sent_ref.dtype)[None], sent_ref.shape)


def slab_body(slab_ref, pieces_ref, new_ref, sent_ref):
    new = next_slab(pieces_ref, slab_ref[...])
    new_ref[...] = new
    sent_ref[...] = jnp.broadcast_to(new.astype(sent_ref.dtype)[None], sent_ref.shape)


def last_slab_body(*refs):
    slab_refs, (pieces_ref, new_ref, sent_ref, table_ref) = refs[:ITERS], refs[ITERS:]
    slabs = [ref[...] for ref in slab_refs]
    new = next_slab(pieces_ref, slabs[-1])
    new_ref[...] = new
    sent_ref[...] = new.astype(sent_ref.dtype)
    slabs.append(new)
    lane = lax.broadcasted_iota(jnp.int32, (1, 128), 1)
    table = jnp.zeros((1, 128), jnp.float32)
    for place, (i, j) in enumerate(PAIRS):
        value = jnp.sum(jnp.sum(slabs[i] * slabs[j], axis=0, keepdims=True), axis=1, keepdims=True)
        table = table + jnp.where(lane == place, value, 0.0)
    table_ref[...] = jnp.broadcast_to(table[None], table_ref.shape)


def fold_body(tables_ref, out_ref):
    out_ref[...] = jnp.broadcast_to(
        jnp.sum(tables_ref[...], axis=0, keepdims=True), out_ref.shape
    )


def dot32(a, b, dims):
    return lax.dot_general(
        a, b, (dims, ((), ())), precision=highest, preferred_element_type=jnp.float32
    )


def four_pivots(p):
    a0, a1, a2 = p(0, 0), p(1, 0), p(1, 1)
    scale = 1.0 / (a0 * a2 - a1 * a1)
    a0, a1, a2 = a2 * scale, -a1 * scale, a0 * scale
    b00, b01, b10, b11 = p(2, 0), p(3, 0), p(2, 1), p(3, 1)
    x00, x01 = a0 * b00 + a1 * b10, a0 * b01 + a1 * b11
    x10, x11 = a1 * b00 + a2 * b10, a1 * b01 + a2 * b11
    s0 = p(2, 2) - (b00 * x00 + b10 * x10)
    s1 = p(3, 2) - (b00 * x01 + b10 * x11)
    s2 = p(3, 3) - (b01 * x01 + b11 * x11)
    scale = 1.0 / (s0 * s2 - s1 * s1)
    s0, s1, s2 = s2 * scale, -s1 * scale, s0 * scale

    def solve(x):
        low0 = x[2] - (x00 * x[0] + x10 * x[1])
        low1 = x[3] - (x01 * x[0] + x11 * x[1])
        y2, y3 = s0 * low0 + s1 * low1, s1 * low0 + s2 * low1
        y0 = (a0 * x[0] + a1 * x[1]) - (x00 * y2 + x01 * y3)
        y1 = (a1 * x[0] + a2 * x[1]) - (x10 * y2 + x11 * y3)
        return [y0, y1, y2, y3]

    return solve


def tree_sum(parts):
    while len(parts) > 1:
        parts = [sum(parts[i + 1 : i + 2], parts[i]) for i in range(0, len(parts), 2)]
    return parts[0]


def inverse_of(block):
    size = block.shape[0]
    lane = lax.broadcasted_iota(jnp.int32, block.shape, 1)
    row = lax.broadcasted_iota(jnp.int32, (PANEL, size), 0)
    panel_lane = lane[:PANEL]
    for k in range(0, size, PANEL):
        cols = [jnp.broadcast_to(block[:, k + i : k + i + 1], block.shape) for i in range(PANEL)]
        inside = (panel_lane >= k) & (panel_lane < k + PANEL)
        unit = jnp.where(panel_lane == row + k, -1.0, 0.0)
        rows = jnp.where(inside, unit, block[k : k + PANEL, :])
        pivots = [col[k : k + PANEL, :] for col in cols]
        for i in range(0, PANEL, 4):
            solve = four_pivots(lambda r, c: pivots[i + c][i + r : i + r + 1])

            def solved(x):
                new = solve([x[i + j : i + j + 1] for j in range(4)])
                y = x - tree_sum([pivots[i + j] * new[j] for j in range(4)])
                for j in range(4):
                    y = jnp.where(row == i + j, new[j], y)
                return y

            rows = solved(rows)
            pivots = [solved(x) if j >= i + 4 else x for j, x in enumerate(pivots)]
        change = tree_sum([col * rows[i : i + 1] for i, col in enumerate(cols)])
        block = jnp.where((lane >= k) & (lane < k + PANEL), 0.0, block) - change
        pieces = [block[:k]] * (k > 0) + [rows] + [block[k + PANEL :]] * (k + PANEL < size)
        block = jnp.concatenate(pieces, axis=0)
    return -block


def weights_of(sums_ref, entries):
    summed = jnp.sum(sums_ref[...], axis=0)
    table = {}
    for place, (i, j) in enumerate(PAIRS):
        table[i, j] = table[j, i] = summed[:, place : place + 1]

    def inner(a, b):
        return tree_sum([x * tree_sum([y * table[i, j] for j, y in enumerate(b)]) for i, x in enumerate(a)])

    def scale_of(squares):
        return lax.rsqrt(squares / entries + epsilon)

    weights = [scale_of(table[0, 0])]
    for _ in range(ITERS):
        up = [0.0 * weights[0]] + [x * (1.0 / SHRINK) for x in weights]
        padded = weights + [0.0 * weights[0]]
        image = [(x - y) * (1.0 / step_size) for x, y in zip(padded, up)]
        rayleigh = inner(weights, image) / (inner(weights, weights) + epsilon)
        update = [y + step_size * rayleigh * x for x, y in zip(padded, up)]
        scale = scale_of(jnp.maximum(inner(update, update), 0.0))
        weights = [x * scale for x in update]
    return weights


def truncate_body(block_rows_ref, ranks_ref, sums_ref, guess_ref, *refs):
    powers = refs[: ITERS - 1]
    last = refs[ITERS - 1 : ITERS + 4]
    slabs = refs[ITERS + 4 : 2 * ITERS + 5]
    slab_ref, cut_ref, state, gram = refs[2 * ITERS + 5 :]
    sector = own_sector()
    slab_rows, width = slab_ref.shape
    capacity = guess_ref.shape[0]
    members = capacity // slab_rows
    weights = weights_of(sums_ref, float(MEAN * block_rows_ref.shape[0] * width))
    live = row_index(guess_ref.shape) < block_rows_ref[sector]
    current = jnp.where(live, guess_ref[...], 0.0) * weights[0]
    for weight, ref in zip(weights[1:], powers):
        current = current + weight * ref[...].astype(jnp.float32)
    state[...] = current
    member = lax.axis_index("mpo")
    own, before, after, far_before, far_after = last
    pieces = [(own, 0), (before, -1), (after, 1)]
    pieces += [(far_before.at[i], -4 + i) for i in range(3)]
    pieces += [(far_after.at[i], 2 + i) for i in range(2)]
    for piece, by in pieces:
        place = lax.rem(member + by + members, members)
        span = pl.ds(pl.multiple_of(place * slab_rows, 8), slab_rows)
        state[span, :] += weights[-1] * piece[...].astype(jnp.float32)
    current = state[...]
    density = dot32(current, current, ((0,), (0,)))
    row = lax.broadcasted_iota(jnp.int32, density.shape, 0)
    lane = lax.broadcasted_iota(jnp.int32, density.shape, 1)
    diagonal = (row == lane).astype(jnp.float32)
    kept = lane < ranks_ref[sector]
    basis = jnp.where(kept, diagonal + density * (1.0 / MEAN), 0.0)
    gram[...] = dot32(basis, basis, ((0,), (0,))) + jnp.where(kept, 0.0, diagonal)
    panel_row = lax.broadcasted_iota(jnp.int32, (BASE, width), 0)
    panel_lane = lax.broadcasted_iota(jnp.int32, (BASE, width), 1)
    for low in range(0, width, BASE):
        panel = gram[low : low + BASE, :]
        inverse = inverse_of(panel[:, low : low + BASE])
        inside = (panel_lane >= low) & (panel_lane < low + BASE)
        select = (panel_lane == panel_row + low).astype(jnp.float32)
        rest = jnp.where(inside, 0.0, panel)
        solved = dot32(inverse, rest, ((1,), (0,)))
        change = dot32(
            jnp.concatenate([rest, solved], axis=0),
            jnp.concatenate([solved, -select], axis=0),
            ((0,), (0,)),
        )
        taken = (lane >= low) & (lane < low + BASE)
        gram[...] = jnp.where(taken, 0.0, gram[...]) - change
        gram[low : low + BASE, :] = solved - dot32(inverse, select, ((1,), (0,)))
    slab = weights[0] * slabs[0][...]
    for weight, ref in zip(weights[1:], slabs[1:]):
        slab = slab + weight * ref[...]
    slab_ref[...] = slab
    coords = dot32(slab, basis, ((1,), (0,)))
    solved = -dot32(coords, gram[...], ((1,), (0,)))
    cut_ref[...] = dot32(solved, basis, ((1,), (1,)))


def passed_along(array, by):
    peers = lax.axis_size("sec")
    return lax.ppermute(array, "sec", [(i, (i + by) % peers) for i in range(peers)])


def swapped(array):
    peers = lax.axis_size("sec")
    return lax.ppermute(array, "sec", [(i, i ^ 1) for i in range(peers)])


def shards(guess, left_env, right_env, block_rows, charges, ranks):
    capacity, width = guess.shape
    sectors = block_rows.shape[0]
    members = lax.axis_size("mpo")
    rows = capacity // members
    exact = like((rows, width), jnp.float32)
    sent = like((members, rows, width), jnp.bfloat16)

    def exchanged(array, axis):
        return lax.all_to_all(array, axis, 0, 0, tiled=True)

    def along(array, by):
        return lax.ppermute(array, "mpo", [(i, (i + by) % members) for i in range(members)])

    whole = begin(block_rows, guess)
    powers, slabs = [], []
    for repeat in range(ITERS - 1):
        part = apply_terms(block_rows, charges, whole, left_env, right_env)
        pieces = exchanged(part.reshape(members, rows, width), "mpo")
        if repeat == 0:
            start, new, outgoing = call(
                first_slab_body, "first_slab", (exact, exact, sent), [SMEM, VMEM, VMEM]
            )(block_rows, guess, pieces)
            slabs.append(start)
        else:
            new, outgoing = call(slab_body, "slab", (exact, sent), [VMEM] * 2)(slabs[-1], pieces)
        slabs.append(new)
        whole = exchanged(outgoing, "mpo").reshape(capacity, width)
        powers.append(whole)
    part = apply_terms(block_rows, charges, whole, left_env, right_env)
    pieces = exchanged(part.reshape(members, rows, width), "mpo")
    new, own, tables = call(
        last_slab_body,
        "last_slab",
        (exact, like((rows, width), jnp.bfloat16), like((sectors, 1, 128), jnp.float32)),
        [VMEM] * (ITERS + 1),
    )(*slabs, pieces)
    slabs.append(new)
    before, after = along(own, 1), along(own, -1)
    before, after, sums = lax.optimization_barrier((before, after, exchanged(tables, "sec")))
    far_before = along(jnp.stack([before, own, after]), 3)
    far_after = along(jnp.stack([before, own]), -3)
    sums = call(fold_body, "fold", like((members, 1, 128), jnp.float32), [VMEM])(sums)
    sums = exchanged(sums, "mpo")
    return call(
        truncate_body,
        "truncate",
        (exact, exact),
        [SMEM, SMEM] + [VMEM] * (2 * ITERS + 7),
        [pltpu.VMEM((capacity, width), jnp.float32), pltpu.VMEM((width, width), jnp.float32)],
        limit=24,
    )(block_rows, ranks, sums, guess, *powers, own, before, after, far_before, far_after, *slabs)


def solution(mesh):
    return jax.shard_map(
        shards,
        mesh=mesh,
        in_specs=(P("sec", None), P("mpo", "sec", None), P("mpo", "sec", None), P(), P("mpo"), P()),
        out_specs=(P(("sec", "mpo"), None), P(("sec", "mpo"), None)),
        check_vma=False,
    )
```

```python
import jax
import jax.numpy as jnp
from jax import lax
from jax.experimental import pallas as pl
from jax.experimental.pallas import tpu as pltpu
from jax.sharding import PartitionSpec as P

MEAN = 256
ITERS = 4
REACH = 2
SHRINK = 2.0**-4
epsilon = 1e-06
step_size = 0.1
highest = lax.Precision.HIGHEST
TILE = 256
BASE = 64
PANEL = 16
PAIRS = [(i, j) for i in range(ITERS + 1) for j in range(i, ITERS + 1)]
SMEM = pl.BlockSpec(memory_space=pltpu.SMEM)
VMEM = pl.BlockSpec(memory_space=pltpu.VMEM)


def call(body, name, out_shape, in_specs, scratch=(), limit=16):
    return pl.pallas_call(
        body,
        in_specs=in_specs,
        out_specs=jax.tree.map(lambda _: VMEM, out_shape),
        out_shape=out_shape,
        scratch_shapes=list(scratch),
        compiler_params=pltpu.CompilerParams(vmem_limit_bytes=limit << 20),
        name=name,
    )


def like(shape, dtype):
    return jax.ShapeDtypeStruct(shape, dtype)


def own_sector():
    return lax.axis_index("sec")


def row_index(shape, base=0):
    return base + lax.broadcasted_iota(jnp.int32, shape, len(shape) - 2)


def begin_body(block_rows_ref, guess_ref, out_ref):
    live = row_index(guess_ref.shape) < block_rows_ref[own_sector()]
    out_ref[...] = jnp.where(live, guess_ref[...], 0.0).astype(out_ref.dtype)


def begin(block_rows, guess):
    return call(begin_body, "begin", like(guess.shape, jnp.bfloat16), [SMEM, VMEM])(
        block_rows, guess
    )


def tile_cases(rows, tiles):
    cases = []
    for i in range(1, tiles + 1):
        fits = rows > (i - 1) * TILE
        cases.append((i * TILE, fits if i == tiles else fits & (rows <= i * TILE)))
    return cases


def middle_of(left, block):
    return jnp.dot(left, block, preferred_element_type=jnp.float32).astype(jnp.bfloat16)


def term_of(charges_ref, charge):
    place = 0
    for term in range(1, charges_ref.shape[0]):
        place = jnp.where(charges_ref[term] == charge, term, place)
    return place


def middle_into(target, block_rows_ref, charges_ref, charge, block_ref, left_ref):
    sector = own_sector()
    sectors = block_rows_ref.shape[0]
    source_rows = block_rows_ref[lax.rem(sector - charge + sectors, sectors)]
    term = term_of(charges_ref, charge)
    tiles = left_ref.shape[1] // TILE
    for high, own_fits in tile_cases(block_rows_ref[sector], tiles):
        for wide, source_fits in tile_cases(source_rows, tiles):

            @pl.when(own_fits & source_fits)
            def _():
                target[:high, :] = middle_of(left_ref[term, :high, :wide], block_ref[:wide, :])


def own_term_body(block_rows_ref, charges_ref, own_ref, left_ref, out_ref):
    term = term_of(charges_ref, 0)
    tiles = left_ref.shape[1] // TILE
    for high, fits in tile_cases(block_rows_ref[own_sector()], tiles):

        @pl.when(fits)
        def _():
            out_ref[:high, :] = middle_of(left_ref[term, :high, :high], own_ref[:high, :])


def summed(pairs, right_ref, high):
    total = 0.0
    for middle, term in pairs:
        total = total + jnp.dot(
            middle[:high, :], right_ref[term], preferred_element_type=jnp.float32
        )
    return total


def far_terms_body(
    block_rows_ref, charges_ref, done_ref, ahead_ref, behind_ref, left_ref, right_ref, out_ref,
    ahead_middle, behind_middle,
):
    middle_into(ahead_middle, block_rows_ref, charges_ref, -REACH, ahead_ref, left_ref)
    middle_into(behind_middle, block_rows_ref, charges_ref, REACH, behind_ref, left_ref)
    pairs = [(done_ref, 0), (ahead_middle, -REACH), (behind_middle, REACH)]
    pairs = [(middle, term_of(charges_ref, charge)) for middle, charge in pairs]
    for high, fits in tile_cases(block_rows_ref[own_sector()], left_ref.shape[1] // TILE):

        @pl.when(fits)
        def _():
            out_ref[:high, :] = summed(pairs, right_ref, high)


def near_terms_body(
    block_rows_ref, charges_ref, sum_ref, partner_ref, other_ref, left_ref, right_ref, out_ref,
    partner_middle, other_middle,
):
    sector = own_sector()
    near = jnp.where(lax.rem(sector, 2) == 0, -1, 1)
    middle_into(partner_middle, block_rows_ref, charges_ref, near, partner_ref, left_ref)
    middle_into(other_middle, block_rows_ref, charges_ref, -near, other_ref, left_ref)
    pairs = [
        (partner_middle, term_of(charges_ref, near)),
        (other_middle, term_of(charges_ref, -near)),
    ]
    capacity, width = out_ref.shape
    own_rows = block_rows_ref[sector]
    for high, fits in tile_cases(own_rows, capacity // TILE):

        @pl.when(fits)
        def _():
            total = sum_ref[:high, :] + summed(pairs, right_ref, high)
            live = row_index(total.shape) < own_rows
            out_ref[:high, :] = jnp.where(live, total, 0.0).astype(out_ref.dtype)
            if high < capacity:
                out_ref[high:, :] = jnp.zeros((capacity - high, width), out_ref.dtype)


def apply_terms(block_rows, charges, whole, left_env, right_env):
    terms, capacity, _ = left_env.shape
    width = right_env.shape[-1]
    block = like((capacity, width), jnp.bfloat16)
    middles = [pltpu.VMEM((capacity, width), jnp.bfloat16)] * 2
    ahead, behind = passed_along(whole, -2), passed_along(whole, 2)
    done = call(own_term_body, "own_term", block, [SMEM, SMEM] + [VMEM] * 2)(
        block_rows, charges, whole, left_env
    )
    whole, done, ahead, behind = lax.optimization_barrier((whole, done, ahead, behind))
    partner = swapped(whole)
    other = swapped(jnp.where(own_sector() % 2 == 0, ahead, behind))
    partial = call(
        far_terms_body,
        "far_terms",
        like((capacity, width), jnp.float32),
        [SMEM, SMEM] + [VMEM] * 5,
        middles,
    )(block_rows, charges, done, ahead, behind, left_env, right_env)
    return call(near_terms_body, "near_terms", block, [SMEM, SMEM] + [VMEM] * 5, middles)(
        block_rows, charges, partial, partner, other, left_env, right_env
    )


def next_slab(pieces_ref, slab):
    applied = jnp.sum(pieces_ref[...].astype(jnp.float32), axis=0)
    return (slab - step_size * applied) * SHRINK


def first_slab_body(block_rows_ref, guess_ref, pieces_ref, start_ref, new_ref, sent_ref):
    rows = start_ref.shape[0]
    base = pl.multiple_of(lax.axis_index("mpo") * rows, 8)
    slab = guess_ref[pl.ds(base, rows), :]
    slab = jnp.where(row_index(slab.shape, base) < block_rows_ref[own_sector()], slab, 0.0)
    start_ref[...] = slab
    new = next_slab(pieces_ref, slab)
    new_ref[...] = new
    sent_ref[...] = jnp.broadcast_to(new.astype(sent_ref.dtype)[None], sent_ref.shape)


def slab_body(slab_ref, pieces_ref, new_ref, sent_ref):
    new = next_slab(pieces_ref, slab_ref[...])
    new_ref[...] = new
    sent_ref[...] = jnp.broadcast_to(new.astype(sent_ref.dtype)[None], sent_ref.shape)


def last_slab_body(*refs):
    slab_refs, (pieces_ref, new_ref, sent_ref, table_ref) = refs[:ITERS], refs[ITERS:]
    slabs = [ref[...] for ref in slab_refs]
    new = next_slab(pieces_ref, slabs[-1])
    new_ref[...] = new
    sent_ref[...] = new.astype(sent_ref.dtype)
    slabs.append(new)
    lane = lax.broadcasted_iota(jnp.int32, (1, 128), 1)
    table = jnp.zeros((1, 128), jnp.float32)
    for place, (i, j) in enumerate(PAIRS):
        value = jnp.sum(jnp.sum(slabs[i] * slabs[j], axis=0, keepdims=True), axis=1, keepdims=True)
        table = table + jnp.where(lane == place, value, 0.0)
    table_ref[...] = jnp.broadcast_to(table[None], table_ref.shape)


def fold_body(tables_ref, out_ref):
    out_ref[...] = jnp.broadcast_to(
        jnp.sum(tables_ref[...], axis=0, keepdims=True), out_ref.shape
    )


def dot32(a, b, dims):
    return lax.dot_general(
        a, b, (dims, ((), ())), precision=highest, preferred_element_type=jnp.float32
    )


def four_pivots(p):
    a0, a1, a2 = p(0, 0), p(1, 0), p(1, 1)
    scale = 1.0 / (a0 * a2 - a1 * a1)
    a0, a1, a2 = a2 * scale, -a1 * scale, a0 * scale
    b00, b01, b10, b11 = p(2, 0), p(3, 0), p(2, 1), p(3, 1)
    x00, x01 = a0 * b00 + a1 * b10, a0 * b01 + a1 * b11
    x10, x11 = a1 * b00 + a2 * b10, a1 * b01 + a2 * b11
    s0 = p(2, 2) - (b00 * x00 + b10 * x10)
    s1 = p(3, 2) - (b00 * x01 + b10 * x11)
    s2 = p(3, 3) - (b01 * x01 + b11 * x11)
    scale = 1.0 / (s0 * s2 - s1 * s1)
    s0, s1, s2 = s2 * scale, -s1 * scale, s0 * scale

    def solve(x):
        low0 = x[2] - (x00 * x[0] + x10 * x[1])
        low1 = x[3] - (x01 * x[0] + x11 * x[1])
        y2, y3 = s0 * low0 + s1 * low1, s1 * low0 + s2 * low1
        y0 = (a0 * x[0] + a1 * x[1]) - (x00 * y2 + x01 * y3)
        y1 = (a1 * x[0] + a2 * x[1]) - (x10 * y2 + x11 * y3)
        return [y0, y1, y2, y3]

    return solve


def tree_sum(parts):
    while len(parts) > 1:
        parts = [sum(parts[i + 1 : i + 2], parts[i]) for i in range(0, len(parts), 2)]
    return parts[0]


def inverse_of(block):
    size = block.shape[0]
    lane = lax.broadcasted_iota(jnp.int32, block.shape, 1)
    row = lax.broadcasted_iota(jnp.int32, (PANEL, size), 0)
    panel_lane = lane[:PANEL]
    for k in range(0, size, PANEL):
        cols = [jnp.broadcast_to(block[:, k + i : k + i + 1], block.shape) for i in range(PANEL)]
        inside = (panel_lane >= k) & (panel_lane < k + PANEL)
        unit = jnp.where(panel_lane == row + k, -1.0, 0.0)
        rows = jnp.where(inside, unit, block[k : k + PANEL, :])
        pivots = [col[k : k + PANEL, :] for col in cols]
        for i in range(0, PANEL, 4):
            solve = four_pivots(lambda r, c: pivots[i + c][i + r : i + r + 1])

            def solved(x):
                new = solve([x[i + j : i + j + 1] for j in range(4)])
                y = x - tree_sum([pivots[i + j] * new[j] for j in range(4)])
                for j in range(4):
                    y = jnp.where(row == i + j, new[j], y)
                return y

            rows = solved(rows)
            pivots = [solved(x) if j >= i + 4 else x for j, x in enumerate(pivots)]
        change = tree_sum([col * rows[i : i + 1] for i, col in enumerate(cols)])
        block = jnp.where((lane >= k) & (lane < k + PANEL), 0.0, block) - change
        pieces = [block[:k]] * (k > 0) + [rows] + [block[k + PANEL :]] * (k + PANEL < size)
        block = jnp.concatenate(pieces, axis=0)
    return -block


def weights_of(sums_ref, entries):
    summed = jnp.sum(sums_ref[...], axis=0)
    table = {}
    for place, (i, j) in enumerate(PAIRS):
        table[i, j] = table[j, i] = summed[:, place : place + 1]

    def inner(a, b):
        return tree_sum([x * tree_sum([y * table[i, j] for j, y in enumerate(b)]) for i, x in enumerate(a)])

    def scale_of(squares):
        return lax.rsqrt(squares / entries + epsilon)

    weights = [scale_of(table[0, 0])]
    for _ in range(ITERS):
        up = [0.0 * weights[0]] + [x * (1.0 / SHRINK) for x in weights]
        padded = weights + [0.0 * weights[0]]
        image = [(x - y) * (1.0 / step_size) for x, y in zip(padded, up)]
        rayleigh = inner(weights, image) / (inner(weights, weights) + epsilon)
        update = [y + step_size * rayleigh * x for x, y in zip(padded, up)]
        scale = scale_of(jnp.maximum(inner(update, update), 0.0))
        weights = [x * scale for x in update]
    return weights


def truncate_body(block_rows_ref, ranks_ref, sums_ref, guess_ref, *refs):
    powers = refs[: ITERS - 1]
    last = refs[ITERS - 1 : ITERS + 4]
    slabs = refs[ITERS + 4 : 2 * ITERS + 5]
    slab_ref, cut_ref, state, gram = refs[2 * ITERS + 5 :]
    sector = own_sector()
    slab_rows, width = slab_ref.shape
    capacity = guess_ref.shape[0]
    members = capacity // slab_rows
    weights = weights_of(sums_ref, float(MEAN * block_rows_ref.shape[0] * width))
    live = row_index(guess_ref.shape) < block_rows_ref[sector]
    current = jnp.where(live, guess_ref[...], 0.0) * weights[0]
    for weight, ref in zip(weights[1:], powers):
        current = current + weight * ref[...].astype(jnp.float32)
    state[...] = current
    member = lax.axis_index("mpo")
    own, before, after, far_before, far_after = last
    pieces = [(own, 0), (before, -1), (after, 1)]
    pieces += [(far_before.at[i], -4 + i) for i in range(3)]
    pieces += [(far_after.at[i], 2 + i) for i in range(2)]
    for piece, by in pieces:
        place = lax.rem(member + by + members, members)
        span = pl.ds(pl.multiple_of(place * slab_rows, 8), slab_rows)
        state[span, :] += weights[-1] * piece[...].astype(jnp.float32)
    current = state[...]
    density = dot32(current, current, ((0,), (0,)))
    row = lax.broadcasted_iota(jnp.int32, density.shape, 0)
    lane = lax.broadcasted_iota(jnp.int32, density.shape, 1)
    diagonal = (row == lane).astype(jnp.float32)
    kept = lane < ranks_ref[sector]
    basis = jnp.where(kept, diagonal + density * (1.0 / MEAN), 0.0)
    gram[...] = dot32(basis, basis, ((0,), (0,))) + jnp.where(kept, 0.0, diagonal)
    panel_row = lax.broadcasted_iota(jnp.int32, (BASE, width), 0)
    panel_lane = lax.broadcasted_iota(jnp.int32, (BASE, width), 1)
    for low in range(0, width, BASE):
        panel = gram[low : low + BASE, :]
        inverse = inverse_of(panel[:, low : low + BASE])
        inside = (panel_lane >= low) & (panel_lane < low + BASE)
        select = (panel_lane == panel_row + low).astype(jnp.float32)
        rest = jnp.where(inside, 0.0, panel)
        solved = dot32(inverse, rest, ((1,), (0,)))
        change = dot32(
            jnp.concatenate([rest, solved], axis=0),
            jnp.concatenate([solved, -select], axis=0),
            ((0,), (0,)),
        )
        taken = (lane >= low) & (lane < low + BASE)
        gram[...] = jnp.where(taken, 0.0, gram[...]) - change
        gram[low : low + BASE, :] = solved - dot32(inverse, select, ((1,), (0,)))
    slab = weights[0] * slabs[0][...]
    for weight, ref in zip(weights[1:], slabs[1:]):
        slab = slab + weight * ref[...]
    slab_ref[...] = slab
    coords = dot32(slab, basis, ((1,), (0,)))
    solved = -dot32(coords, gram[...], ((1,), (0,)))
    cut_ref[...] = dot32(solved, basis, ((1,), (1,)))


def passed_along(array, by):
    peers = lax.axis_size("sec")
    return lax.ppermute(array, "sec", [(i, (i + by) % peers) for i in range(peers)])


def swapped(array):
    peers = lax.axis_size("sec")
    return lax.ppermute(array, "sec", [(i, i ^ 1) for i in range(peers)])


def shards(guess, left_env, right_env, block_rows, charges, ranks):
    capacity, width = guess.shape
    sectors = block_rows.shape[0]
    members = lax.axis_size("mpo")
    rows = capacity // members
    exact = like((rows, width), jnp.float32)
    sent = like((members, rows, width), jnp.bfloat16)

    def exchanged(array, axis):
        return lax.all_to_all(array, axis, 0, 0, tiled=True)

    def along(array, by):
        return lax.ppermute(array, "mpo", [(i, (i + by) % members) for i in range(members)])

    whole = begin(block_rows, guess)
    powers, slabs = [], []
    for repeat in range(ITERS - 1):
        part = apply_terms(block_rows, charges, whole, left_env, right_env)
        pieces = exchanged(part.reshape(members, rows, width), "mpo")
        if repeat == 0:
            start, new, outgoing = call(
                first_slab_body, "first_slab", (exact, exact, sent), [SMEM, VMEM, VMEM]
            )(block_rows, guess, pieces)
            slabs.append(start)
        else:
            new, outgoing = call(slab_body, "slab", (exact, sent), [VMEM] * 2)(slabs[-1], pieces)
        slabs.append(new)
        whole = exchanged(outgoing, "mpo").reshape(capacity, width)
        powers.append(whole)
    part = apply_terms(block_rows, charges, whole, left_env, right_env)
    pieces = exchanged(part.reshape(members, rows, width), "mpo")
    new, own, tables = call(
        last_slab_body,
        "last_slab",
        (exact, like((rows, width), jnp.bfloat16), like((sectors, 1, 128), jnp.float32)),
        [VMEM] * (ITERS + 1),
    )(*slabs, pieces)
    slabs.append(new)
    before, after = along(own, 1), along(own, -1)
    before, after, sums = lax.optimization_barrier((before, after, exchanged(tables, "sec")))
    far_before = along(jnp.stack([before, own, after]), 3)
    far_after = along(jnp.stack([before, own]), -3)
    sums = call(fold_body, "fold", like((members, 1, 128), jnp.float32), [VMEM])(sums)
    sums = exchanged(sums, "mpo")
    return call(
        truncate_body,
        "truncate",
        (exact, exact),
        [SMEM, SMEM] + [VMEM] * (2 * ITERS + 7),
        [pltpu.VMEM((capacity, width), jnp.float32), pltpu.VMEM((width, width), jnp.float32)],
        limit=24,
    )(block_rows, ranks, sums, guess, *powers, own, before, after, far_before, far_after, *slabs)


def solution(mesh):
    return jax.shard_map(
        shards,
        mesh=mesh,
        in_specs=(P("sec", None), P("mpo", "sec", None), P("mpo", "sec", None), P(), P("mpo"), P()),
        out_specs=(P(("sec", "mpo"), None), P(("sec", "mpo"), None)),
        check_vma=False,
    )
```
